32 devices in a mesh: groups: 2 (over x), wide: 16 (over z, y, core).
Axes of the slice: x: 2, y: 2, z: 4, core: 2. Of those that a mesh axis runs over, the one named last changes fastest.
Arguments:
- prefix_hidden: bfloat16 [32, 256, 8192], P(('groups', 'wide')), parts along dimension 0, may hold values from -6 to 6
- prefix_lengths: int32 [32], P(('groups', 'wide')), parts along dimension 0, may hold values from 64 to 256
- action_noise: float32 [32, 50, 32], P(('groups', 'wide')), parts along dimension 0, may hold values from -4 to 4
- prefix_gain: float32 [8192], replicated, may hold values from 0.1 to 1.9
- key_weight: bfloat16 [8192, 512], P('wide'), may hold values from -0.0625 to 0.0625
- value_weight: bfloat16 [8192, 512], P('wide'), may hold values from -0.0625 to 0.0625
- input_weight: float32 [32, 1024], replicated, may hold values from -1 to 1
- expert_gain: float32 [1024], replicated, may hold values from 0.1 to 1.9
- expert_query: bfloat16 [1024, 1024], P('wide'), may hold values from -0.1875 to 0.1875
- expert_key: bfloat16 [1024, 512], P('wide'), may hold values from -5.3125 to 5.3125
- expert_value: bfloat16 [1024, 512], P('wide'), may hold values from -0.1875 to 0.1875
- expert_output: bfloat16 [1024, 1024], P('wide'), may hold values from -0.1875 to 0.1875
- final_gain: float32 [1024], replicated, may hold values from 0.1 to 1.9
- output_weight: bfloat16 [1024, 32], replicated, may hold values from -0.1875 to 0.1875
Outputs:
- actions: float32 [32, 50, 32], P(('groups', 'wide')), parts along dimension 0
The draws below stay inside these ranges and needn't reach their ends.
There are 2 independent parts, one for each index of `groups`. The reference program is written for one: setup_inputs(seed, part) draws one part's arguments, and reference() takes and returns one part's arrays. A program takes and returns all parts, laid end to end along the dimension named above; an argument that names none is the same for every part. Nothing has to cross between parts.
Inputs may be any that keep to these rules, and one draw needn't show every extreme that they name: `prefix_lengths`: positions at or after a sample's length are padding and take no part.
All inputs are finite; a program needn't handle non-finite values.
Results may differ from the reference program's by a relative error of at most 0.0075.
Values may be sent and summed in bfloat16 or wider, within the bound.
No kernel may reach another device: no remote copies, remote signals or barrier semaphores. Data moves between devices by JAX's collectives and lax.ppermute only.
A program may use at most 128 MiB of HBM per device.

```python
import jax
import jax.numpy as jnp
from jax import lax

D = 8192
HEAD = 128
KV_HEADS = 4
ACT_WIDTH = 1024
ACT_HEADS = 8
ACT_DIM = 32
SPAN = 50
STEPS = 4
PREFIX = 256
SAMPLES = 16
KV = 512
QUERY_WIDTH = 1024


def coupled_weights(key):
    query_seed = jax.random.fold_in(key, 71)
    other_seed = jax.random.fold_in(key, 72)
    scale_factor = ACT_WIDTH ** (-0.5)
    query_draw = jnp.clip(jax.random.normal(query_seed, (ACT_WIDTH, ACT_HEADS * HEAD), jnp.float32), -6.0, 6.0) * scale_factor
    key_draw = jnp.clip(jax.random.normal(other_seed, (ACT_WIDTH, KV_HEADS * HEAD), jnp.float32), -6.0, 6.0) * scale_factor
    return (query_draw, key_draw)


def draw_expert_query(key, part):
    return coupled_weights(key)[0].astype(jnp.bfloat16)


def draw_expert_key(key, part):
    return coupled_weights(key)[1].astype(jnp.bfloat16)


def draw_action_noise(key, part):
    base_rows = jnp.clip(jax.random.normal(key, (SAMPLES, SPAN, ACT_DIM), jnp.float32), -4.0, 4.0)
    return base_rows


def touch_ends(array, rng, low, top_value):
    longest = array.shape.index(max(array.shape))
    spots = []
    for shift in (0, 1):
        where = [jax.random.randint(jax.random.fold_in(rng, axis), (), 0, length) for axis, length in enumerate(array.shape)]
        where[longest] = (where[longest] + shift) % array.shape[longest]
        spots.append(tuple(where))
    return array.at[spots[0]].set(low).at[spots[1]].set(top_value)


def levels(rng, dims, cuts, low, largest):
    level = 1.0
    for dim, parts in cuts:
        draws = jax.random.uniform(jax.random.fold_in(jax.random.fold_in(rng, 6), dim), (parts,), jnp.float32, low / len(cuts), largest / len(cuts))
        level = level * jnp.repeat(jnp.exp(draws), dims[dim] // parts).reshape((-1,) + (1,) * (len(dims) - 1 - dim))
    return level


def gaussian(key, shape, width, limit, pieces=(), kind=jnp.bfloat16):
    factor_of = levels(key, shape, pieces, -0.22, 0.18) if pieces else 1.0
    array = jax.random.normal(key, shape, jnp.float32) * width * factor_of
    return jnp.minimum(jnp.maximum(array, -limit), limit).astype(kind)


def setup_inputs(seed: int = 0, part: int = 0) -> dict:
    seeds = jax.random.split(jax.random.key(seed), 15)
    part_keys = jax.random.split(jax.random.fold_in(seeds[14], part), 15)
    return {
        "prefix_hidden": gaussian(part_keys[0], (SAMPLES, PREFIX, D), 1.0, 6.0, ((0, 16),)),
        "prefix_lengths": touch_ends(jax.random.randint(part_keys[1], (SAMPLES,), PREFIX // 4, PREFIX + 1), jax.random.fold_in(part_keys[1], 1), PREFIX // 4, PREFIX).astype(jnp.int32),
        "action_noise": draw_action_noise(jax.random.fold_in(jax.random.fold_in(seeds[14], part), 71), part),
        "prefix_gain": jnp.clip(1.0 + 0.18 * jax.random.normal(seeds[3], (D,), jnp.float32), 0.1, 1.9),
        "key_weight": gaussian(seeds[4], (D, KV), D ** -0.5, 0.0625, ((0, 16),)),
        "value_weight": gaussian(seeds[5], (D, KV), D ** -0.5, 0.0625, ((0, 16),)),
        "input_weight": gaussian(seeds[6], (ACT_DIM, ACT_WIDTH), ACT_DIM ** -0.5, 1.0, (), jnp.float32),
        "expert_gain": jnp.clip(1.0 + 0.18 * jax.random.normal(seeds[7], (ACT_WIDTH,), jnp.float32), 0.1, 1.9),
        "expert_query": draw_expert_query(jax.random.fold_in(seeds[14], 71), part),
        "expert_key": draw_expert_key(jax.random.fold_in(seeds[14], 71), part),
        "expert_value": gaussian(seeds[10], (ACT_WIDTH, KV), ACT_WIDTH ** -0.5, 0.1875, ((0, 16),)),
        "expert_output": gaussian(seeds[11], (QUERY_WIDTH, ACT_WIDTH), QUERY_WIDTH ** -0.5, 0.1875, ((0, 16),)),
        "final_gain": jnp.clip(1.0 + 0.18 * jax.random.normal(seeds[12], (ACT_WIDTH,), jnp.float32), 0.1, 1.9),
        "output_weight": gaussian(seeds[13], (ACT_WIDTH, ACT_DIM), ACT_WIDTH ** -0.5, 0.1875),
    }


rope_base = 1000000.0
norm_eps = 1e-06

def normalize(values, norm_gain):
    mean_square = lax.optimization_barrier(jnp.mean(values * values, axis=-1, keepdims=True))
    return values * lax.rsqrt(mean_square + norm_eps) * norm_gain

def rotate(values, positions):
    half_width = values.shape[-1] // 2
    inv_freqs = rope_base ** (-jnp.arange(half_width, dtype=jnp.float32) * 2.0 / values.shape[-1])
    angles = positions[:, None] * inv_freqs[None, :]
    cosine = jnp.cos(angles)[:, None, :]
    sine_part = jnp.sin(angles)[:, None, :]
    first_half = values[..., :half_width]
    second = values[..., half_width:]
    return jnp.concatenate([first_half * cosine - second * sine_part, second * cosine + first_half * sine_part], -1)

def time_embedding(time_value, embed_width):
    half_width = embed_width // 2
    fraction = jnp.arange(half_width, dtype=jnp.float32) / (half_width - 1)
    period = 0.004 * (4.0 / 0.004) ** fraction
    angles = time_value * (2.0 * jnp.pi) / period
    return jnp.concatenate([jnp.sin(angles), jnp.cos(angles)])

def attend(queries, key_cache, value_cache, action_keys, action_values, is_valid):
    span_rows = queries.shape[0]
    groups = key_cache.shape[1] // HEAD
    group_ratio = queries.shape[1] // key_cache.shape[1]
    query_heads = queries.reshape(span_rows, groups, group_ratio, HEAD).astype(jnp.float32)
    prefix_keys = key_cache.reshape(-1, groups, HEAD).astype(jnp.float32)
    prefix_values = value_cache.reshape(-1, groups, HEAD).astype(jnp.float32)
    own_keys = action_keys.reshape(span_rows, groups, HEAD).astype(jnp.float32)
    own_values = action_values.reshape(span_rows, groups, HEAD).astype(jnp.float32)
    prefix_scores = jnp.einsum('cgrh,pgh->grcp', query_heads, prefix_keys)
    prefix_scores = jnp.where(is_valid[None, None, None, :], prefix_scores, -1e+30)
    own_scores = jnp.einsum('cgrh,ngh->grcn', query_heads, own_keys)
    row_max = jnp.maximum(lax.optimization_barrier(jnp.max(prefix_scores, -1)), lax.optimization_barrier(jnp.max(own_scores, -1)))[..., None]
    prefix_exp = jnp.exp(prefix_scores - row_max)
    own_exp = jnp.exp(own_scores - row_max)
    prob_total = lax.optimization_barrier(jnp.sum(prefix_exp, -1, keepdims=True)) + lax.optimization_barrier(jnp.sum(own_exp, -1, keepdims=True))
    prefix_prob = (prefix_exp / prob_total).astype(jnp.bfloat16).astype(jnp.float32)
    own_prob = (own_exp / prob_total).astype(jnp.bfloat16).astype(jnp.float32)
    attn_mixed = jnp.einsum('grcp,pgh->cgrh', prefix_prob, prefix_values) + jnp.einsum('grcn,ngh->cgrh', own_prob, own_values)
    return attn_mixed.reshape(span_rows, -1).astype(jnp.bfloat16)

def prefill_one(hidden, prefix_gain, key_weight, value_weight):
    row_count = hidden.shape[0]
    normed = normalize(hidden.astype(jnp.float32), prefix_gain).astype(jnp.bfloat16)
    raw_keys = jnp.dot(normed, key_weight, preferred_element_type=jnp.float32)
    raw_values = jnp.dot(normed, value_weight, preferred_element_type=jnp.float32)
    positions = jnp.arange(row_count, dtype=jnp.float32)
    key_cache = rotate(raw_keys.reshape(row_count, -1, HEAD), positions).reshape(row_count, -1).astype(jnp.bfloat16)
    return (key_cache, raw_values.astype(jnp.bfloat16))

def expert_steps(noise_rows, length, input_weight, expert_gain, query_w, key_w, value_w, output_w, final_gain, output_weight, key_cache, value_cache):
    span_rows = noise_rows.shape[0]
    is_valid = jnp.arange(key_cache.shape[0], dtype=jnp.int32) < length
    positions = length.astype(jnp.float32) + jnp.arange(span_rows, dtype=jnp.float32)
    action_state = noise_rows
    for step_idx in range(STEPS):
        time_value = 1.0 - step_idx / STEPS
        hidden = jnp.dot(action_state, input_weight, precision=lax.Precision.HIGHEST, preferred_element_type=jnp.float32)
        hidden = hidden + time_embedding(time_value, input_weight.shape[1])[None, :]
        normed = normalize(hidden, expert_gain).astype(jnp.bfloat16)
        raw_queries = jnp.dot(normed, query_w, preferred_element_type=jnp.float32)
        queries = rotate(raw_queries.reshape(span_rows, -1, HEAD), positions).reshape(span_rows, -1)
        queries = (queries * HEAD ** (-0.5)).astype(jnp.bfloat16)
        raw_keys = jnp.dot(normed, key_w, preferred_element_type=jnp.float32)
        action_keys = rotate(raw_keys.reshape(span_rows, -1, HEAD), positions).reshape(span_rows, -1).astype(jnp.bfloat16)
        action_values = jnp.dot(normed, value_w, preferred_element_type=jnp.float32).astype(jnp.bfloat16)
        attn_mixed = attend(queries, key_cache, value_cache, action_keys, action_values, is_valid)
        hidden = hidden + jnp.dot(attn_mixed, output_w, preferred_element_type=jnp.float32)
        final_normed = normalize(hidden, final_gain).astype(jnp.bfloat16)
        velocity = jnp.dot(final_normed, output_weight, preferred_element_type=jnp.float32)
        action_state = action_state - velocity / STEPS
    return action_state

def reference(prefix_hidden, prefix_lengths, action_noise, prefix_gain, key_weight, value_weight, input_weight, expert_gain, expert_query, expert_key, expert_value, expert_output, final_gain, output_weight):

    def one_sample(sample_args):
        hidden, length, noise_rows = sample_args
        key_cache, value_cache = prefill_one(hidden, prefix_gain, key_weight, value_weight)
        return expert_steps(noise_rows, length, input_weight, expert_gain, expert_query, expert_key, expert_value, expert_output, final_gain, output_weight, key_cache, value_cache)
    return lax.map(one_sample, (prefix_hidden, prefix_lengths, action_noise))
```

```python
import functools

import jax
import jax.numpy as jnp
from jax import lax
from jax.experimental import pallas as pl
from jax.experimental.pallas import tpu as pltpu
from jax.sharding import PartitionSpec as P

HEAD = 128
STEPS = 4

rope_base = 1000000.0
norm_eps = 1e-06

ANY = pl.BlockSpec(memory_space=pl.ANY)
SMEM = pl.BlockSpec(memory_space=pltpu.SMEM)
VMEM = pl.BlockSpec(memory_space=pltpu.VMEM)


def rope_tables(positions, scale=1.0):
    half_width = HEAD // 2
    inv_freqs = rope_base ** (-jnp.arange(half_width, dtype=jnp.float32) * 2.0 / HEAD)
    angles = positions[:, None] * inv_freqs[None, :]
    cosine = jnp.cos(angles) * scale
    sine_part = jnp.sin(angles) * scale
    return (
        jnp.concatenate([cosine, cosine], -1),
        jnp.concatenate([-sine_part, sine_part], -1),
    )


def time_embedding(time_value, embed_width):
    half_width = embed_width // 2
    fraction = jnp.arange(half_width, dtype=jnp.float32) / (half_width - 1)
    period = 0.004 * (4.0 / 0.004) ** fraction
    angles = time_value * (2.0 * jnp.pi) / period
    return jnp.concatenate([jnp.sin(angles), jnp.cos(angles)])


def norm_kernel(picks, hidden_ref, gain_ref, *outs, chips, width):
    rows = hidden_ref[...].astype(jnp.float32)
    scale = lax.rsqrt(jnp.mean(rows * rows, axis=-1, keepdims=True) + norm_eps)
    for which, out in enumerate(outs):
        for chip in range(chips):
            start = pl.multiple_of((chip * 4 + picks[which]) * width, width)
            part = hidden_ref[:, pl.ds(start, width)].astype(jnp.float32)
            part = part * scale * gain_ref[:, pl.ds(start, width)]
            out[:, chip * width : (chip + 1) * width] = part.astype(jnp.bfloat16)


def norm_parts(hidden, gain, picks, chips):
    row_count, depth = hidden.shape
    width = depth // chips // 4
    if width % HEAD:
        wide = hidden.astype(jnp.float32)
        scale = lax.rsqrt(jnp.mean(wide * wide, axis=-1, keepdims=True) + norm_eps)
        parts = (wide * scale * gain).astype(jnp.bfloat16).reshape(row_count, chips, 4, width)
        return tuple(
            lax.dynamic_index_in_dim(parts, picks[k], 2, keepdims=False).reshape(row_count, -1)
            for k in range(4)
        )
    step = 64
    shape = jax.ShapeDtypeStruct((row_count, depth // 4), jnp.bfloat16)
    return pl.pallas_call(
        functools.partial(norm_kernel, chips=chips, width=width),
        grid_spec=pltpu.PrefetchScalarGridSpec(
            num_scalar_prefetch=1,
            grid=(row_count // step,),
            in_specs=[
                pl.BlockSpec((step, depth), lambda i, p: (i, 0)),
                pl.BlockSpec((1, depth), lambda i, p: (0, 0)),
            ],
            out_specs=[pl.BlockSpec((step, depth // 4), lambda i, p: (i, 0))] * 4,
        ),
        out_shape=[shape] * 4,
        name="prefix_norm",
    )(picks, hidden, gain[None, :])


def project_kernel(spots, first, second, *refs, count, width):
    pieces = refs[:count]
    first_out, second_out, weight, sems = refs[count:]
    copies = []
    for k, piece in enumerate(pieces):
        start = pl.multiple_of(spots[k] * width, width)
        copy = pltpu.make_async_copy(piece, weight.at[pl.ds(start, width)], sems.at[k])
        copy.start()
        copies.append(copy)
    for copy in copies:
        copy.wait()
    first_out[...] = jnp.dot(first[...], weight[...], preferred_element_type=jnp.float32)
    second_out[...] = jnp.dot(second[...], weight[...], preferred_element_type=jnp.float32)


def project(spots, first, second, pieces):
    width, columns = pieces[0].shape
    shape = jax.ShapeDtypeStruct((first.shape[0], columns), jnp.float32)
    return pl.pallas_call(
        functools.partial(project_kernel, count=len(pieces), width=width),
        in_specs=[SMEM, VMEM, VMEM] + [ANY] * len(pieces),
        out_specs=[VMEM, VMEM],
        out_shape=[shape, shape],
        scratch_shapes=[
            pltpu.VMEM((width * len(pieces), columns), jnp.bfloat16),
            pltpu.SemaphoreType.DMA((len(pieces),)),
        ],
        name="prefix_project",
    )(spots, first, second, *pieces)


def turn(values, cosine, sine):
    return values * cosine + pltpu.roll(values, HEAD // 2, 1) * sine


def expert_kernel(
    info,
    noise,
    input_weight,
    embed,
    expert_gain,
    final_gain,
    output_weight,
    query_cos,
    query_sin,
    action_cos,
    action_sin,
    prefix_cos,
    prefix_sin,
    kept,
    paired,
    twinned,
    *refs,
    span,
    heads,
    groups,
    proj_count,
    proj_rows,
    out_count,
    out_rows,
):
    proj_pieces = refs[:proj_count]
    out_pieces = refs[proj_count : proj_count + out_count]
    actions, proj, mix, key_cache, value_cache, joined, sems = refs[proj_count + out_count :]
    copies = []
    for k, piece in enumerate(proj_pieces):
        start = pl.multiple_of(info[1 + k] * proj_rows, proj_rows)
        copies.append(
            pltpu.make_async_copy(piece, proj.at[pl.ds(start, proj_rows)], sems.at[k])
        )
    late = []
    for k, piece in enumerate(out_pieces):
        for part in range(2):
            slot = 2 * k + part
            start = pl.multiple_of(info[1 + proj_count + slot] * out_rows, out_rows)
            late.append(
                pltpu.make_async_copy(
                    piece.at[pl.ds(part * out_rows, out_rows)],
                    mix.at[pl.ds(start, out_rows)],
                    sems.at[proj_count + slot],
                )
            )
    for copy in copies + late:
        copy.start()
    length = info[0]
    kv_width = groups * HEAD
    for g in range(groups):
        cut = slice(g * HEAD, (g + 1) * HEAD)
        raw = kept[:, cut] + paired[:, cut] + twinned[:, cut].astype(jnp.float32)
        key_cache[:, cut] = turn(raw, prefix_cos[...], prefix_sin[...]).astype(jnp.bfloat16)
        cut2 = slice(kv_width + g * HEAD, kv_width + (g + 1) * HEAD)
        raw = kept[:, cut2] + paired[:, cut2] + twinned[:, cut2].astype(jnp.float32)
        value_cache[:, cut] = raw.astype(jnp.bfloat16)
    for copy in copies + late:
        copy.wait()
    ratio = heads // groups
    rows = noise.shape[0]
    query_width = heads * HEAD
    contract = (((1,), (1,)), ((), ()))
    prefix_ok = lax.broadcasted_iota(jnp.int32, (1, key_cache.shape[0]), 1) < length
    own_ok = lax.broadcasted_iota(jnp.int32, (1, rows), 1) < span
    actions[...] = noise[...]

    def step(k, carry):
        state = actions[...]
        hidden = jnp.dot(
            state,
            input_weight[...],
            precision=lax.Precision.HIGHEST,
            preferred_element_type=jnp.float32,
        )
        hidden = hidden + embed[pl.ds(k, 1), :]
        square = jnp.mean(hidden * hidden, axis=-1, keepdims=True)
        normed = (hidden * lax.rsqrt(square + norm_eps) * expert_gain[...]).astype(jnp.bfloat16)
        raw = jnp.dot(normed, proj[...], preferred_element_type=jnp.float32)
        for g in range(groups):
            cut = slice(g * HEAD, (g + 1) * HEAD)
            own_keys = turn(
                raw[:, query_width + g * HEAD : query_width + (g + 1) * HEAD],
                action_cos[...],
                action_sin[...],
            ).astype(jnp.bfloat16)
            base = query_width + kv_width
            own_values = raw[:, base + g * HEAD : base + (g + 1) * HEAD].astype(jnp.bfloat16)
            queries = jnp.concatenate(
                [
                    turn(
                        raw[:, (g * ratio + r) * HEAD : (g * ratio + r + 1) * HEAD],
                        query_cos[...],
                        query_sin[...],
                    ).astype(jnp.bfloat16)
                    for r in range(ratio)
                ],
                0,
            )
            far = lax.dot_general(
                queries, key_cache[:, cut], contract, preferred_element_type=jnp.float32
            )
            near = lax.dot_general(queries, own_keys, contract, preferred_element_type=jnp.float32)
            far = jnp.where(prefix_ok, far, -1e30)
            near = jnp.where(own_ok, near, -1e30)
            row_max = jnp.maximum(
                jnp.max(far, -1, keepdims=True), jnp.max(near, -1, keepdims=True)
            )
            far = jnp.exp(far - row_max)
            near = jnp.exp(near - row_max)
            total = jnp.sum(far, -1, keepdims=True) + jnp.sum(near, -1, keepdims=True)
            inverse = 1.0 / total
            far = (far * inverse).astype(jnp.bfloat16)
            near = (near * inverse).astype(jnp.bfloat16)
            mixed = jnp.dot(far, value_cache[:, cut], preferred_element_type=jnp.float32)
            mixed = mixed + jnp.dot(near, own_values, preferred_element_type=jnp.float32)
            mixed = mixed.astype(jnp.bfloat16)
            for r in range(ratio):
                h = g * ratio + r
                joined[:, h * HEAD : (h + 1) * HEAD] = mixed[r * rows : (r + 1) * rows]
        hidden = hidden + jnp.dot(joined[...], mix[...], preferred_element_type=jnp.float32)
        square = jnp.mean(hidden * hidden, axis=-1, keepdims=True)
        normed = (hidden * lax.rsqrt(square + norm_eps) * final_gain[...]).astype(jnp.bfloat16)
        velocity = jnp.dot(normed, output_weight[...], preferred_element_type=jnp.float32)
        actions[...] = state - velocity / STEPS
        return carry

    lax.fori_loop(0, STEPS, step, 0)


def expert(info, dense, proj_pieces, out_pieces, span, groups):
    proj_rows, proj_width = proj_pieces[0].shape
    out_rows = out_pieces[0].shape[0] // 2
    noise = dense[0]
    prefix = dense[12].shape[0]
    proj_depth = proj_rows * len(proj_pieces)
    out_depth = out_rows * 2 * len(out_pieces)
    out_width = out_pieces[0].shape[1]
    heads = out_depth // HEAD
    return pl.pallas_call(
        functools.partial(
            expert_kernel,
            span=span,
            heads=heads,
            groups=groups,
            proj_count=len(proj_pieces),
            proj_rows=proj_rows,
            out_count=len(out_pieces),
            out_rows=out_rows,
        ),
        in_specs=[SMEM] + [VMEM] * len(dense) + [ANY] * (len(proj_pieces) + len(out_pieces)),
        out_specs=VMEM,
        out_shape=jax.ShapeDtypeStruct(noise.shape, jnp.float32),
        scratch_shapes=[
            pltpu.VMEM((proj_depth, proj_width), jnp.bfloat16),
            pltpu.VMEM((out_depth, out_width), jnp.bfloat16),
            pltpu.VMEM((prefix, groups * HEAD), jnp.bfloat16),
            pltpu.VMEM((prefix, groups * HEAD), jnp.bfloat16),
            pltpu.VMEM((noise.shape[0], heads * HEAD), jnp.bfloat16),
            pltpu.SemaphoreType.DMA((len(proj_pieces) + 2 * len(out_pieces),)),
        ],
        name="expert_steps",
    )(info, *dense, *proj_pieces, *out_pieces)


def shards(
    prefix_hidden,
    prefix_lengths,
    action_noise,
    prefix_gain,
    key_weight,
    value_weight,
    input_weight,
    expert_gain,
    expert_query,
    expert_key,
    expert_value,
    expert_output,
    final_gain,
    output_weight,
    *,
    group_count,
    wide_count,
):
    chips = wide_count // 2
    columns = chips // 2
    place = lax.axis_index("wide")
    core = place % 2
    row = place // 2 % 2
    column = place // 4
    twin = lax.axis_index("groups") % 2
    ring = [(w, (w + 4) % wide_count) for w in range(wide_count)]
    across = [(w, w ^ 2) for w in range(wide_count)]
    beside = [(w, w ^ 1) for w in range(wide_count)]
    facing = [(g, g ^ 1) for g in range(group_count)]
    corner = [
        (g * wide_count + w, (g ^ 1) * wide_count + (w ^ 1))
        for g in range(group_count)
        for w in range(wide_count)
    ]

    def round_ring(piece):
        slots = [piece]
        for _ in range(columns - 1):
            slots.append(lax.ppermute(slots[-1], "wide", ring))
        return slots

    def over(piece):
        return lax.ppermute(piece, "wide", across)

    def swap(piece):
        return lax.ppermute(piece, "wide", beside)

    half = key_weight.shape[0] // 2
    mine = jnp.concatenate(
        [
            lax.dynamic_slice_in_dim(key_weight, twin * half, half, 0),
            lax.dynamic_slice_in_dim(value_weight, twin * half, half, 0),
        ],
        1,
    )
    kv_slots = round_ring(mine)
    kv_pieces = kv_slots + [over(piece) for piece in kv_slots]

    own = core * 2 + twin
    picks = jnp.stack([own, own ^ 2, own ^ 1, own ^ 3]).astype(jnp.int32)
    kept, to_core, to_twin, to_corner = norm_parts(
        prefix_hidden[0], prefix_gain, picks, chips
    )
    from_twin = lax.ppermute(to_twin, "groups", facing)
    from_corner = lax.ppermute(to_corner, ("groups", "wide"), corner)
    from_core = swap(to_core)

    proj_slots = round_ring(jnp.concatenate([expert_query, expert_key, expert_value], 1))
    proj_pieces = proj_slots + [over(piece) for piece in proj_slots]
    proj_pieces = proj_pieces + [swap(piece) for piece in proj_pieces]
    out_pieces = round_ring(jnp.concatenate([expert_output, over(expert_output)], 0))
    out_pieces = out_pieces + [swap(piece) for piece in out_pieces]

    ring_columns = [(column - s) % columns for s in range(columns)]
    near_spots = [c * 2 + row for c in ring_columns] + [c * 2 + 1 - row for c in ring_columns]
    spots = jnp.stack(near_spots).astype(jnp.int32)
    own_part, core_part = project(spots, kept, from_core, kv_pieces)
    twin_part, corner_part = project(spots, from_twin, from_corner, kv_pieces)
    own_paired = swap(core_part)
    twin_sum = (twin_part + swap(corner_part)).astype(jnp.bfloat16)
    twinned = lax.ppermute(twin_sum, "groups", facing)

    proj_spots = [s * 2 + core for s in near_spots] + [s * 2 + 1 - core for s in near_spots]
    out_spots = []
    for side in (core, 1 - core):
        for c in ring_columns:
            out_spots += [(c * 2 + row) * 2 + side, (c * 2 + 1 - row) * 2 + side]
    length = prefix_lengths[0]
    info = jnp.stack([length] + proj_spots + out_spots).astype(jnp.int32)

    span, _ = action_noise.shape[1:]
    rows = -(-span // 16) * 16
    noise = jnp.pad(action_noise[0], ((0, rows - span), (0, 0)))
    embed = jnp.stack(
        [time_embedding(1.0 - k / STEPS, input_weight.shape[1]) for k in range(STEPS)]
    )
    positions = length.astype(jnp.float32) + jnp.arange(rows, dtype=jnp.float32)
    query_cos, query_sin = rope_tables(positions, HEAD ** (-0.5))
    action_cos, action_sin = rope_tables(positions)
    prefix_cos, prefix_sin = rope_tables(
        jnp.arange(prefix_hidden.shape[1], dtype=jnp.float32)
    )
    dense = (
        noise,
        input_weight,
        embed,
        expert_gain[None, :],
        final_gain[None, :],
        output_weight,
        query_cos,
        query_sin,
        action_cos,
        action_sin,
        prefix_cos,
        prefix_sin,
        own_part,
        own_paired,
        twinned,
    )
    groups = key_weight.shape[1] // HEAD
    actions = expert(info, dense, proj_pieces, out_pieces, span, groups)
    return actions[None, :span]


def solution(mesh):
    placed = (
        P(("groups", "wide"), None, None),
        P(("groups", "wide")),
        P(("groups", "wide"), None, None),
        P(),
        P("wide", None),
        P("wide", None),
        P(),
        P(),
        P("wide", None),
        P("wide", None),
        P("wide", None),
        P("wide", None),
        P(),
        P(),
    )
    return jax.shard_map(
        functools.partial(
            shards, group_count=mesh.shape["groups"], wide_count=mesh.shape["wide"]
        ),
        mesh=mesh,
        in_specs=placed,
        out_specs=P(("groups", "wide"), None, None),
        check_vma=False,
    )
```

```python
import functools

import jax
import jax.numpy as jnp
from jax import lax
from jax.experimental import pallas as pl
from jax.experimental.pallas import tpu as pltpu
from jax.sharding import PartitionSpec as P


HEAD = 128
STEPS = 4

rope_base = 1000000.0
norm_eps = 1e-06


ANY = pl.BlockSpec(memory_space=pl.ANY)
SMEM = pl.BlockSpec(memory_space=pltpu.SMEM)
VMEM = pl.BlockSpec(memory_space=pltpu.VMEM)


def rope_tables(positions, scale=1.0):
    half_width = HEAD // 2
    inv_freqs = rope_base ** (-jnp.arange(half_width, dtype=jnp.float32) * 2.0 / HEAD)
    angles = positions[:, None] * inv_freqs[None, :]
    cosine = jnp.cos(angles) * scale
    sine_part = jnp.sin(angles) * scale
    return (
        jnp.concatenate([cosine, cosine], -1),
        jnp.concatenate([-sine_part, sine_part], -1),
    )


def time_embedding(time_value, embed_width):
    half_width = embed_width // 2
    fraction = jnp.arange(half_width, dtype=jnp.float32) / (half_width - 1)
    period = 0.004 * (4.0 / 0.004) ** fraction
    angles = time_value * (2.0 * jnp.pi) / period
    return jnp.concatenate([jnp.sin(angles), jnp.cos(angles)])


def places():
    place = lax.axis_index("wide")
    core = lax.rem(place, 2)
    row = lax.rem(lax.div(place, 2), 2)
    column = lax.div(place, 4)
    twin = lax.rem(lax.axis_index("groups"), 2)
    return core, row, column, twin


def chip_spots(row, column, columns):
    ring = [lax.rem(column + (columns - s), columns) for s in range(columns)]
    return [c * 2 + row for c in ring] + [c * 2 + (1 - row) for c in ring]


def pick_kernel(hidden, out, sems, *, flip, chips, width):
    core, _, _, twin = places()
    core = 1 - core if flip & 2 else core
    twin = 1 - twin if flip & 1 else twin
    part = core * 2 + twin
    copies = []
    for chip in range(chips):
        start = pl.multiple_of((chip * 4 + part) * width, width)
        copies.append(
            pltpu.make_async_copy(
                hidden.at[:, pl.ds(start, width)],
                out.at[:, pl.ds(chip * width, width)],
                sems.at[chip],
            )
        )
    for copy in copies:
        copy.start()
    for copy in copies:
        copy.wait()


def pick(hidden, flip, chips):
    row_count, depth = hidden.shape
    width = depth // chips // 4
    if width % HEAD:
        core, _, _, twin = places()
        part = (core * 2 + twin) ^ flip
        parts = hidden.reshape(row_count, chips, 4, width)
        return lax.dynamic_index_in_dim(parts, part, 2, keepdims=False).reshape(row_count, -1)
    return pl.pallas_call(
        functools.partial(pick_kernel, flip=flip, chips=chips, width=width),
        in_specs=[ANY],
        out_specs=VMEM,
        out_shape=jax.ShapeDtypeStruct((row_count, depth // 4), jnp.bfloat16),
        scratch_shapes=[pltpu.SemaphoreType.DMA((chips,))],
        name="pick_columns",
    )(hidden)


def own_kernel(hidden, kept, row_scale, *, chips, width):
    core, _, _, twin = places()
    part = core * 2 + twin
    rows = hidden[...].astype(jnp.float32)
    row_scale[...] = lax.rsqrt(jnp.mean(rows * rows, axis=-1, keepdims=True) + norm_eps)
    for chip in range(chips):
        start = pl.multiple_of((chip * 4 + part) * width, width)
        kept[:, chip * width : (chip + 1) * width] = hidden[:, pl.ds(start, width)]


def own_part_and_scale(hidden, chips):
    row_count, depth = hidden.shape
    width = depth // chips // 4
    if width % HEAD:
        rows = hidden.astype(jnp.float32)
        scale = lax.rsqrt(jnp.mean(rows * rows, axis=-1, keepdims=True) + norm_eps)
        return pick(hidden, 0, chips), scale
    step = 64
    return pl.pallas_call(
        functools.partial(own_kernel, chips=chips, width=width),
        grid=(row_count // step,),
        in_specs=[pl.BlockSpec((step, depth), lambda i: (i, 0))],
        out_specs=[
            pl.BlockSpec((step, depth // 4), lambda i: (i, 0)),
            pl.BlockSpec((step, 1), lambda i: (i, 0)),
        ],
        out_shape=[
            jax.ShapeDtypeStruct((row_count, depth // 4), jnp.bfloat16),
            jax.ShapeDtypeStruct((row_count, 1), jnp.float32),
        ],
        name="own_part",
    )(hidden)


def project_kernel(first, second, *refs, count, width, columns):
    keys = refs[:count]
    values = refs[count : 2 * count]
    first_out, second_out, rows, weight, sems = refs[2 * count :]
    _, row, column, _ = places()
    spots = chip_spots(row, column, columns)
    half = first.shape[0]
    split = weight.shape[1] // 2
    row_copies = [
        pltpu.make_async_copy(first, rows.at[pl.ds(0, half)], sems.at[2 * count]),
        pltpu.make_async_copy(second, rows.at[pl.ds(half, half)], sems.at[2 * count + 1]),
    ]
    copies = []
    for side, pieces in enumerate((keys, values)):
        for k, piece in enumerate(pieces):
            start = pl.multiple_of(spots[k] * width, width)
            copies.append(
                pltpu.make_async_copy(
                    piece,
                    weight.at[pl.ds(start, width), pl.ds(side * split, split)],
                    sems.at[side * count + k],
                )
            )
    for copy in row_copies + copies:
        copy.start()
    for copy in row_copies:
        copy.wait()
    for side in range(2):
        for copy in copies[side * count : (side + 1) * count]:
            copy.wait()
        cut = slice(side * split, (side + 1) * split)
        for out, start in ((first_out, 0), (second_out, half)):
            out[:, cut] = jnp.dot(
                rows[start : start + half], weight[:, cut], preferred_element_type=jnp.float32
            )


def project(first, second, keys, values, columns):
    width, split = keys[0].shape
    half, depth = first.shape
    count = len(keys)
    shape = jax.ShapeDtypeStruct((half, 2 * split), jnp.float32)
    return pl.pallas_call(
        functools.partial(project_kernel, count=count, width=width, columns=columns),
        in_specs=[ANY] * (2 + 2 * count),
        out_specs=[VMEM, VMEM],
        out_shape=[shape, shape],
        scratch_shapes=[
            pltpu.VMEM((2 * half, depth), jnp.bfloat16),
            pltpu.VMEM((depth, 2 * split), jnp.bfloat16),
            pltpu.SemaphoreType.DMA((2 * count + 2,)),
        ],
        name="prefix_project",
    )(first, second, *keys, *values)


def turn(values, cosine, sine):
    return values * cosine + pltpu.roll(values, HEAD // 2, 1) * sine


def expert_kernel(
    lengths,
    noise,
    input_weight,
    embed,
    expert_gain,
    final_gain,
    output_weight,
    query_cos,
    query_sin,
    action_cos,
    action_sin,
    prefix_cos,
    prefix_sin,
    row_scale,
    kept,
    paired,
    twinned,
    *refs,
    columns,
    span,
    heads,
    groups,
    proj_count,
    proj_rows,
    out_count,
    out_rows,
):
    proj_pieces = refs[:proj_count]
    out_pieces = refs[proj_count : proj_count + out_count]
    (actions, proj, mix, key_cache, value_cache, joined, state_ref, turned, sems) = refs[
        proj_count + out_count :
    ]
    core, row, column, _ = places()
    spots = chip_spots(row, column, columns)
    copies = []
    late = []
    for side in range(2):
        half = 1 - core if side else core
        for k, spot in enumerate(spots):
            piece = proj_pieces[side * len(spots) + k]
            start = pl.multiple_of((spot * 2 + half) * proj_rows, proj_rows)
            copies.append(
                pltpu.make_async_copy(
                    piece, proj.at[pl.ds(start, proj_rows)], sems.at[len(copies)]
                )
            )
        for k, spot in enumerate(spots):
            cross, slot = divmod(k, columns)
            piece = out_pieces[side * columns + slot]
            start = pl.multiple_of((spot * 2 + half) * out_rows, out_rows)
            late.append(
                pltpu.make_async_copy(
                    piece.at[pl.ds(cross * out_rows, out_rows)],
                    mix.at[pl.ds(start, out_rows)],
                    sems.at[proj_count + len(late)],
                )
            )
    for copy in copies + late:
        copy.start()
    length = lengths[0]
    kv_width = groups * HEAD
    for g in range(groups):
        cut = slice(g * HEAD, (g + 1) * HEAD)
        raw = kept[:, cut] + paired[:, cut] + twinned[:, cut].astype(jnp.float32)
        raw = raw * row_scale[...]
        key_cache[:, cut] = turn(raw, prefix_cos[...], prefix_sin[...]).astype(jnp.bfloat16)
        cut2 = slice(kv_width + g * HEAD, kv_width + (g + 1) * HEAD)
        raw = kept[:, cut2] + paired[:, cut2] + twinned[:, cut2].astype(jnp.float32)
        value_cache[:, cut] = (raw * row_scale[...]).astype(jnp.bfloat16)
    for copy in copies + late:
        copy.wait()
    ratio = heads // groups
    rows = joined.shape[0]
    query_width = heads * HEAD
    contract = (((1,), (1,)), ((), ()))
    prefix_ok = lax.broadcasted_iota(jnp.int32, (1, key_cache.shape[0]), 1) < length
    own_ok = lax.broadcasted_iota(jnp.int32, (1, rows), 1) < span
    turned[...] = jnp.zeros_like(turned)
    turned[:, :span] = noise[...]
    state_ref[...] = turned[...].T

    def step(k, carry):
        state = state_ref[...]
        hidden = jnp.dot(
            state,
            input_weight[...],
            precision=lax.Precision.HIGHEST,
            preferred_element_type=jnp.float32,
        )
        hidden = hidden + embed[pl.ds(k, 1), :]
        square = jnp.mean(hidden * hidden, axis=-1, keepdims=True)
        normed = (hidden * lax.rsqrt(square + norm_eps) * expert_gain[...]).astype(jnp.bfloat16)
        raw = jnp.dot(normed, proj[...], preferred_element_type=jnp.float32)
        for g in range(groups):
            cut = slice(g * HEAD, (g + 1) * HEAD)
            own_keys = turn(
                raw[:, query_width + g * HEAD : query_width + (g + 1) * HEAD],
                action_cos[...],
                action_sin[...],
            ).astype(jnp.bfloat16)
            base = query_width + kv_width
            own_values = raw[:, base + g * HEAD : base + (g + 1) * HEAD].astype(jnp.bfloat16)
            queries = jnp.concatenate(
                [
                    turn(
                        raw[:, (g * ratio + r) * HEAD : (g * ratio + r + 1) * HEAD],
                        query_cos[...],
                        query_sin[...],
                    ).astype(jnp.bfloat16)
                    for r in range(ratio)
                ],
                0,
            )
            far = lax.dot_general(
                queries, key_cache[:, cut], contract, preferred_element_type=jnp.float32
            )
            near = lax.dot_general(queries, own_keys, contract, preferred_element_type=jnp.float32)
            far = jnp.where(prefix_ok, far, -1e30)
            near = jnp.where(own_ok, near, -1e30)
            row_max = jnp.maximum(
                jnp.max(far, -1, keepdims=True), jnp.max(near, -1, keepdims=True)
            )
            far = jnp.exp(far - row_max)
            near = jnp.exp(near - row_max)
            total = jnp.sum(far, -1, keepdims=True) + jnp.sum(near, -1, keepdims=True)
            inverse = 1.0 / total
            far = (far * inverse).astype(jnp.bfloat16)
            near = (near * inverse).astype(jnp.bfloat16)
            mixed = jnp.dot(far, value_cache[:, cut], preferred_element_type=jnp.float32)
            mixed = mixed + jnp.dot(near, own_values, preferred_element_type=jnp.float32)
            mixed = mixed.astype(jnp.bfloat16)
            for r in range(ratio):
                h = g * ratio + r
                joined[:, h * HEAD : (h + 1) * HEAD] = mixed[r * rows : (r + 1) * rows]
        hidden = hidden + jnp.dot(joined[...], mix[...], preferred_element_type=jnp.float32)
        square = jnp.mean(hidden * hidden, axis=-1, keepdims=True)
        normed = (hidden * lax.rsqrt(square + norm_eps) * final_gain[...]).astype(jnp.bfloat16)
        velocity = lax.dot_general(
            normed, output_weight[...], contract, preferred_element_type=jnp.float32
        )
        state_ref[...] = state - velocity / STEPS
        return carry

    lax.fori_loop(0, STEPS, step, 0)
    turned[...] = state_ref[...].T
    actions[...] = turned[:, :span]


def expert(lengths, dense, proj_pieces, out_pieces, columns, span, groups):
    proj_rows, proj_width = proj_pieces[0].shape
    out_rows = out_pieces[0].shape[0] // 2
    noise = dense[0]
    rows = dense[6].shape[0]
    prefix = dense[12].shape[0]
    proj_depth = proj_rows * len(proj_pieces)
    out_depth = out_rows * 2 * len(out_pieces)
    out_width = out_pieces[0].shape[1]
    heads = out_depth // HEAD
    return pl.pallas_call(
        functools.partial(
            expert_kernel,
            columns=columns,
            span=span,
            heads=heads,
            groups=groups,
            proj_count=len(proj_pieces),
            proj_rows=proj_rows,
            out_count=len(out_pieces),
            out_rows=out_rows,
        ),
        in_specs=[SMEM] + [VMEM] * len(dense) + [ANY] * (len(proj_pieces) + len(out_pieces)),
        out_specs=VMEM,
        out_shape=jax.ShapeDtypeStruct(noise.shape, jnp.float32),
        scratch_shapes=[
            pltpu.VMEM((proj_depth, proj_width), jnp.bfloat16),
            pltpu.VMEM((out_depth, out_width), jnp.bfloat16),
            pltpu.VMEM((prefix, groups * HEAD), jnp.bfloat16),
            pltpu.VMEM((prefix, groups * HEAD), jnp.bfloat16),
            pltpu.VMEM((rows, heads * HEAD), jnp.bfloat16),
            pltpu.VMEM((rows, noise.shape[0]), jnp.float32),
            pltpu.VMEM((noise.shape[0], rows), jnp.float32),
            pltpu.SemaphoreType.DMA((len(proj_pieces) + 2 * len(out_pieces),)),
        ],
        name="expert_steps",
    )(lengths, *dense, *proj_pieces, *out_pieces)


def shards(
    prefix_hidden,
    prefix_lengths,
    action_noise,
    prefix_gain,
    key_weight,
    value_weight,
    input_weight,
    expert_gain,
    expert_query,
    expert_key,
    expert_value,
    expert_output,
    final_gain,
    output_weight,
    *,
    group_count,
    wide_count,
):
    chips = wide_count // 2
    columns = chips // 2
    _, _, _, twin = places()
    ring = [(w, (w + 4) % wide_count) for w in range(wide_count)]
    across = [(w, w ^ 2) for w in range(wide_count)]
    beside = [(w, w ^ 1) for w in range(wide_count)]
    facing = [(g, g ^ 1) for g in range(group_count)]
    corner = [
        (g * wide_count + w, (g ^ 1) * wide_count + (w ^ 1))
        for g in range(group_count)
        for w in range(wide_count)
    ]

    def round_ring(piece):
        slots = [piece]
        for _ in range(1, columns):
            slots.append(lax.ppermute(slots[-1], "wide", ring))
        return slots

    def over(slots):
        return [lax.ppermute(slot, "wide", across) for slot in slots]

    def swap(pieces):
        return [lax.ppermute(piece, "wide", beside) for piece in pieces]

    hidden = prefix_hidden[0]
    to_corner = pick(hidden, 3, chips)
    from_corner = lax.ppermute(to_corner, ("groups", "wide"), corner)
    to_twin = pick(hidden, 1, chips)
    from_twin = lax.ppermute(to_twin, "groups", facing)
    to_core = pick(hidden, 2, chips)
    from_core = lax.ppermute(to_core, "wide", beside)
    kept, row_scale = own_part_and_scale(hidden, chips)

    half = key_weight.shape[0] // 2
    place = lax.axis_index("wide")
    gain = lax.dynamic_slice_in_dim(prefix_gain, (place * 2 + twin) * half, half, 0)

    def scaled(weight):
        part = lax.dynamic_slice_in_dim(weight, twin * half, half, 0)
        return (part.astype(jnp.float32) * gain[:, None]).astype(jnp.bfloat16)

    key_slots = round_ring(scaled(key_weight))
    value_slots = round_ring(scaled(value_weight))
    key_pieces = key_slots + over(key_slots)
    value_pieces = value_slots + over(value_slots)

    proj_own = jnp.concatenate([expert_query, expert_key, expert_value], 1)
    length = prefix_lengths[0]
    span = action_noise.shape[1]
    rows = -(-span // 16) * 16
    embed = jnp.stack(
        [time_embedding(1.0 - k / STEPS, input_weight.shape[1]) for k in range(STEPS)]
    )
    positions = length.astype(jnp.float32) + jnp.arange(rows, dtype=jnp.float32)
    tables = (
        embed,
        *rope_tables(positions, HEAD ** (-0.5)),
        *rope_tables(positions),
        *rope_tables(jnp.arange(hidden.shape[0], dtype=jnp.float32)),
    )
    kept, tables = lax.optimization_barrier((kept, tables))

    proj_slots = round_ring(proj_own)
    proj_pieces = proj_slots + over(proj_slots)
    proj_pieces = proj_pieces + swap(proj_pieces)
    out_own = jnp.concatenate([expert_output] + over([expert_output]), 0)
    out_pieces = round_ring(out_own)
    out_pieces = out_pieces + swap(out_pieces)

    corner_part, twin_part = project(
        from_corner, from_twin, key_pieces, value_pieces, columns
    )
    core_part, own_part = project(from_core, kept, key_pieces, value_pieces, columns)
    corner_paired = lax.ppermute(corner_part, "wide", beside)
    twin_sum = (twin_part + corner_paired).astype(jnp.bfloat16)
    twinned = lax.ppermute(twin_sum, "groups", facing)
    own_paired = lax.ppermute(core_part, "wide", beside)

    dense = (
        action_noise[0].T,
        input_weight,
        tables[0],
        expert_gain[None, :],
        final_gain[None, :],
        output_weight.T,
        *tables[1:],
        row_scale,
        own_part,
        own_paired,
        twinned,
    )
    groups = key_weight.shape[1] // HEAD
    actions = expert(
        prefix_lengths, dense, proj_pieces, out_pieces, columns, span, groups
    )
    return actions.T[None]


def solution(mesh):
    placed = (
        P(("groups", "wide"), None, None),
        P(("groups", "wide")),
        P(("groups", "wide"), None, None),
        P(),
        P("wide", None),
        P("wide", None),
        P(),
        P(),
        P("wide", None),
        P("wide", None),
        P("wide", None),
        P("wide", None),
        P(),
        P(),
    )

    def whole(*arrays):
        return shards(
            *arrays, group_count=mesh.shape["groups"], wide_count=mesh.shape["wide"]
        )

    return jax.shard_map(
        whole,
        mesh=mesh,
        in_specs=placed,
        out_specs=P(("groups", "wide"), None, None),
        check_vma=False,
    )
```

```python
import functools

import jax
import jax.numpy as jnp
from jax import lax
from jax.experimental import pallas as pl
from jax.experimental.pallas import tpu as pltpu
from jax.sharding import PartitionSpec as P


HEAD = 128
STEPS = 4

rope_base = 1000000.0
norm_eps = 1e-06


ANY = pl.BlockSpec(memory_space=pl.ANY)
SMEM = pl.BlockSpec(memory_space=pltpu.SMEM)
VMEM = pl.BlockSpec(memory_space=pltpu.VMEM)


def near_memory(pieces):
    return [pltpu.with_memory_space_constraint(piece, pltpu.VMEM) for piece in pieces]


def room(mebibytes):
    return pltpu.CompilerParams(vmem_limit_bytes=mebibytes << 20)


def rope_tables(positions):
    half_width = HEAD // 2
    lane = lax.broadcasted_iota(jnp.int32, (1, HEAD), 1)
    band = (lane % half_width).astype(jnp.float32)
    angles = positions[:, None] * rope_base ** (-band * 2.0 / HEAD)
    sign = jnp.where(lane < half_width, -1.0, 1.0)
    return jnp.cos(angles), jnp.sin(angles) * sign


def time_embeddings(embed_width):
    half_width = embed_width // 2
    lane = lax.broadcasted_iota(jnp.int32, (1, embed_width), 1)
    step = lax.broadcasted_iota(jnp.int32, (STEPS, 1), 0).astype(jnp.float32)
    fraction = (lane % half_width).astype(jnp.float32) / (half_width - 1)
    period = 0.004 * (4.0 / 0.004) ** fraction
    angles = (1.0 - step / STEPS) * (2.0 * jnp.pi) / period
    return jnp.where(lane < half_width, jnp.sin(angles), jnp.cos(angles))


def places():
    place = lax.axis_index("wide")
    core = lax.rem(place, 2)
    row = lax.rem(lax.div(place, 2), 2)
    column = lax.div(place, 4)
    twin = lax.rem(lax.axis_index("groups"), 2)
    return core, row, column, twin


def chip_spots(row, column, columns):
    ring = [lax.rem(column + (columns - s), columns) for s in range(columns)]
    return [c * 2 + row for c in ring] + [c * 2 + (1 - row) for c in ring]


def pick_kernel(hidden, out, staged, sems, *, flip, chips, width):
    core, _, _, twin = places()
    core = 1 - core if flip & 2 else core
    twin = 1 - twin if flip & 1 else twin
    part = core * 2 + twin
    inward = []
    outward = []
    for chip in range(chips):
        start = pl.multiple_of((chip * 4 + part) * width, width)
        here = pl.ds(chip * width, width)
        inward.append(
            pltpu.make_async_copy(
                hidden.at[:, pl.ds(start, width)], staged.at[:, here], sems.at[chip]
            )
        )
        outward.append(
            pltpu.make_async_copy(staged.at[:, here], out.at[:, here], sems.at[chips + chip])
        )
    for copy in inward:
        copy.start()
    for first, second in zip(inward, outward):
        first.wait()
        second.start()
    for copy in outward:
        copy.wait()


def pick(hidden, flip, chips):
    row_count, depth = hidden.shape
    width = depth // chips // 4
    if width % HEAD:
        core, _, _, twin = places()
        part = (core * 2 + twin) ^ flip
        parts = hidden.reshape(row_count, chips, 4, width)
        return lax.dynamic_index_in_dim(parts, part, 2, keepdims=False).reshape(row_count, -1)
    return pl.pallas_call(
        functools.partial(pick_kernel, flip=flip, chips=chips, width=width),
        in_specs=[ANY],
        out_specs=ANY,
        out_shape=jax.ShapeDtypeStruct((row_count, depth // 4), jnp.bfloat16),
        scratch_shapes=[
            pltpu.VMEM((row_count, depth // 4), jnp.bfloat16),
            pltpu.SemaphoreType.DMA((2 * chips,)),
        ],
        compiler_params=room(4),
        name="pick_columns",
    )(hidden)


def own_kernel(hidden, kept, row_scale, *, chips, width):
    core, _, _, twin = places()
    part = core * 2 + twin
    rows = hidden[...].astype(jnp.float32)
    row_scale[...] = lax.rsqrt(jnp.mean(rows * rows, axis=-1, keepdims=True) + norm_eps)
    for chip in range(chips):
        start = pl.multiple_of((chip * 4 + part) * width, width)
        kept[:, chip * width : (chip + 1) * width] = hidden[:, pl.ds(start, width)]


def own_part_and_scale(hidden, chips):
    row_count, depth = hidden.shape
    width = depth // chips // 4
    if width % HEAD:
        rows = hidden.astype(jnp.float32)
        scale = lax.rsqrt(jnp.mean(rows * rows, axis=-1, keepdims=True) + norm_eps)
        return pick(hidden, 0, chips), scale
    step = 64
    return pl.pallas_call(
        functools.partial(own_kernel, chips=chips, width=width),
        grid=(row_count // step,),
        in_specs=[pl.BlockSpec((step, depth), lambda i: (i, 0))],
        out_specs=[
            pl.BlockSpec((step, depth // 4), lambda i: (i, 0)),
            pl.BlockSpec((step, 1), lambda i: (i, 0)),
        ],
        out_shape=[
            jax.ShapeDtypeStruct((row_count, depth // 4), jnp.bfloat16),
            jax.ShapeDtypeStruct((row_count, 1), jnp.float32),
        ],
        compiler_params=room(8),
        name="own_part",
    )(hidden)


def project_kernel(first, second, *refs, count, width, columns):
    keys = refs[:count]
    values = refs[count : 2 * count]
    first_out, second_out, rows, weight, sems = refs[2 * count :]
    _, row, column, _ = places()
    spots = chip_spots(row, column, columns)
    half = first.shape[0]
    split = weight.shape[1] // 2
    row_copies = [
        pltpu.make_async_copy(first, rows.at[pl.ds(0, half)], sems.at[2 * count]),
        pltpu.make_async_copy(second, rows.at[pl.ds(half, half)], sems.at[2 * count + 1]),
    ]
    copies = []
    for side, pieces in enumerate((keys, values)):
        for k, piece in enumerate(pieces):
            start = pl.multiple_of(spots[k] * width, width)
            copies.append(
                pltpu.make_async_copy(
                    piece,
                    weight.at[pl.ds(start, width), pl.ds(side * split, split)],
                    sems.at[side * count + k],
                )
            )
    for copy in row_copies + copies:
        copy.start()
    for copy in row_copies:
        copy.wait()
    for side in range(2):
        for copy in copies[side * count : (side + 1) * count]:
            copy.wait()
        cut = slice(side * split, (side + 1) * split)
        for out, start in ((first_out, 0), (second_out, half)):
            out[:, cut] = jnp.dot(
                rows[start : start + half], weight[:, cut], preferred_element_type=jnp.float32
            )


def project(first, second, keys, values, columns):
    width, split = keys[0].shape
    half, depth = first.shape
    count = len(keys)
    shape = jax.ShapeDtypeStruct((half, 2 * split), jnp.float32)
    return pl.pallas_call(
        functools.partial(project_kernel, count=count, width=width, columns=columns),
        in_specs=[ANY] * 2 + [VMEM] * (2 * count),
        out_specs=[VMEM, VMEM],
        out_shape=[shape, shape],
        scratch_shapes=[
            pltpu.VMEM((2 * half, depth), jnp.bfloat16),
            pltpu.VMEM((depth, 2 * split), jnp.bfloat16),
            pltpu.SemaphoreType.DMA((2 * count + 2,)),
        ],
        compiler_params=room(14),
        name="prefix_project",
    )(first, second, *near_memory(keys), *near_memory(values))


def turn(values, cosine, sine):
    return values * cosine + pltpu.roll(values, HEAD // 2, 1) * sine


SUMS = 3
LEFT_PARTS = (0, 0, 1, 0, 1, 2)
RIGHT_PARTS = (0, 1, 0, 2, 1, 0)


def three_parts(values):
    first = values.astype(jnp.bfloat16)
    rest = values - first.astype(jnp.float32)
    second = rest.astype(jnp.bfloat16)
    third = (rest - second.astype(jnp.float32)).astype(jnp.bfloat16)
    return first, second, third


def expert_kernel(
    lengths,
    noise,
    input_weight,
    embed,
    expert_gain,
    final_gain,
    output_weight,
    cosine,
    sine,
    row_scale,
    *refs,
    columns,
    span,
    heads,
    groups,
    proj_count,
    proj_rows,
    out_count,
    out_rows,
):
    sums = refs[:SUMS]
    refs = refs[SUMS:]
    proj_pieces = refs[:proj_count]
    out_pieces = refs[proj_count : proj_count + out_count]
    (
        actions,
        proj,
        mix,
        keys,
        values,
        joined,
        state_ref,
        turned,
        input_parts,
        output_parts,
        exact,
        rounded,
        sems,
    ) = refs[proj_count + out_count :]
    core, row, column, _ = places()
    spots = chip_spots(row, column, columns)
    prefix = row_scale.shape[0]
    early = []
    late = []
    for side in range(2):
        half = 1 - core if side else core
        for k, spot in enumerate(spots):
            piece = proj_pieces[side * len(spots) + k]
            start = pl.multiple_of((spot * 2 + half) * proj_rows, proj_rows)
            early.append((piece, proj.at[pl.ds(start, proj_rows)]))
        for k, spot in enumerate(spots):
            cross, slot = divmod(k, columns)
            piece = out_pieces[side * columns + slot]
            start = pl.multiple_of((spot * 2 + half) * out_rows, out_rows)
            late.append(
                (piece.at[pl.ds(cross * out_rows, out_rows)], mix.at[pl.ds(start, out_rows)])
            )
    targets = [exact.at[0], exact.at[1], rounded]
    first = list(zip(sums, targets))
    copies = [
        pltpu.make_async_copy(source, target, sems.at[k])
        for k, (source, target) in enumerate(first + early + late)
    ]
    for copy in copies:
        copy.start()
    first, copies = copies[: len(first)], copies[len(first) :]
    early, late = copies[: len(early)], copies[len(early) :]

    width = noise.shape[0]
    weight_parts = three_parts(input_weight[...])
    turned[...] = jnp.zeros_like(turned)
    for k, part in enumerate(RIGHT_PARTS):
        cut = slice(k * width, (k + 1) * width)
        input_parts[cut] = weight_parts[part]
        output_parts[cut] = output_weight[...]
        turned[cut, :span] = noise[...]
    state_ref[...] = turned[...].T
    rows, wide = state_ref.shape
    action_cos = cosine[:rows]
    action_sin = sine[:rows]
    query_cos = action_cos * HEAD ** (-0.5)
    query_sin = action_sin * HEAD ** (-0.5)
    keys[:, prefix + rows :] = jnp.zeros_like(keys[:, prefix + rows :])
    values[:, prefix + rows :] = jnp.zeros_like(values[:, prefix + rows :])

    for copy in first:
        copy.wait()
    for side, out in enumerate((keys, values)):
        for g in range(groups):
            start = (side * groups + g) * HEAD
            cut = slice(start, start + HEAD)
            raw = exact[0, :, cut] + exact[1, :, cut]
            raw = (raw + rounded[:, cut].astype(jnp.float32)) * row_scale[...]
            if side == 0:
                raw = turn(raw, cosine[rows:], sine[rows:])
            out[g, :prefix] = raw.astype(jnp.bfloat16)

    ratio = heads // groups
    query_width = heads * HEAD
    kv_width = groups * HEAD
    contract = (((1,), (1,)), ((), ()))
    place = lax.broadcasted_iota(jnp.int32, (1, keys.shape[1]), 1)
    allowed = (place < lengths[0]) | ((place >= prefix) & (place < prefix + span))
    lane = lax.broadcasted_iota(jnp.int32, (1, wide), 1)
    is_second = (lane < 0)
    is_third = is_second
    for k, part in enumerate(LEFT_PARTS):
        here = (lane >= k * width) & (lane < (k + 1) * width)
        if part == 1:
            is_second = is_second | here
        if part == 2:
            is_third = is_third | here

    def step(k, carry):
        state = state_ref[...]
        first = state.astype(jnp.bfloat16).astype(jnp.float32)
        rest_part = state - first
        second = rest_part.astype(jnp.bfloat16).astype(jnp.float32)
        third = rest_part - second
        parts = jnp.where(is_third, third, jnp.where(is_second, second, first))
        hidden = jnp.dot(
            parts.astype(jnp.bfloat16), input_parts[...], preferred_element_type=jnp.float32
        )
        hidden = hidden + embed[pl.ds(k, 1), :]
        square = jnp.mean(hidden * hidden, axis=-1, keepdims=True)
        normed = (hidden * lax.rsqrt(square + norm_eps) * expert_gain[...]).astype(jnp.bfloat16)

        @pl.when(k == 0)
        def _():
            for copy in early:
                copy.wait()

        raw = jnp.dot(normed, proj[...], preferred_element_type=jnp.float32)

        @pl.when(k == 0)
        def _():
            for copy in late:
                copy.wait()

        base = query_width + kv_width
        for g in range(groups):
            keys[g, prefix : prefix + rows] = turn(
                raw[:, query_width + g * HEAD : query_width + (g + 1) * HEAD],
                action_cos,
                action_sin,
            ).astype(jnp.bfloat16)
            values[g, prefix : prefix + rows] = raw[
                :, base + g * HEAD : base + (g + 1) * HEAD
            ].astype(jnp.bfloat16)
            queries = jnp.concatenate(
                [
                    turn(
                        raw[:, (g * ratio + r) * HEAD : (g * ratio + r + 1) * HEAD],
                        query_cos,
                        query_sin,
                    ).astype(jnp.bfloat16)
                    for r in range(ratio)
                ],
                0,
            )
            scores = lax.dot_general(
                queries, keys[g], contract, preferred_element_type=jnp.float32
            )
            scores = jnp.where(allowed, scores, -1e30)
            scores = jnp.exp(scores - jnp.max(scores, -1, keepdims=True))
            inverse = 1.0 / jnp.sum(scores, -1, keepdims=True)
            mixed = jnp.dot(
                scores.astype(jnp.bfloat16), values[g], preferred_element_type=jnp.float32
            )
            mixed = (mixed * inverse).astype(jnp.bfloat16)
            for r in range(ratio):
                h = g * ratio + r
                joined[:, h * HEAD : (h + 1) * HEAD] = mixed[r * rows : (r + 1) * rows]
        hidden = hidden + jnp.dot(joined[...], mix[...], preferred_element_type=jnp.float32)
        square = jnp.mean(hidden * hidden, axis=-1, keepdims=True)
        normed = (hidden * lax.rsqrt(square + norm_eps) * final_gain[...]).astype(jnp.bfloat16)
        velocity = lax.dot_general(
            normed, output_parts[...], contract, preferred_element_type=jnp.float32
        )
        state_ref[...] = state - velocity / STEPS
        return carry

    lax.fori_loop(0, STEPS, step, 0)
    turned[...] = state_ref[...].T
    actions[...] = turned[:width, :span]


def expert(lengths, dense, sums, proj_pieces, out_pieces, columns, span):
    proj_rows, proj_width = proj_pieces[0].shape
    out_rows = out_pieces[0].shape[0] // 2
    noise = dense[0]
    width = noise.shape[0]
    prefix, sum_width = sums[0].shape
    rows = dense[6].shape[0] - prefix
    groups = sum_width // HEAD // 2
    proj_depth = proj_rows * len(proj_pieces)
    out_depth = out_rows * 2 * len(out_pieces)
    out_width = out_pieces[0].shape[1]
    heads = out_depth // HEAD
    total = -(-(prefix + rows) // HEAD) * HEAD
    stack = len(LEFT_PARTS)
    return pl.pallas_call(
        functools.partial(
            expert_kernel,
            columns=columns,
            span=span,
            heads=heads,
            groups=groups,
            proj_count=len(proj_pieces),
            proj_rows=proj_rows,
            out_count=len(out_pieces),
            out_rows=out_rows,
        ),
        in_specs=[SMEM]
        + [VMEM] * len(dense)
        + [VMEM] * (len(sums) + len(proj_pieces) + len(out_pieces)),
        out_specs=VMEM,
        out_shape=jax.ShapeDtypeStruct(noise.shape, jnp.float32),
        scratch_shapes=[
            pltpu.VMEM((proj_depth, proj_width), jnp.bfloat16),
            pltpu.VMEM((out_depth, out_width), jnp.bfloat16),
            pltpu.VMEM((groups, total, HEAD), jnp.bfloat16),
            pltpu.VMEM((groups, total, HEAD), jnp.bfloat16),
            pltpu.VMEM((rows, heads * HEAD), jnp.bfloat16),
            pltpu.VMEM((rows, stack * width), jnp.float32),
            pltpu.VMEM((stack * width, rows), jnp.float32),
            pltpu.VMEM((stack * width, out_width), jnp.bfloat16),
            pltpu.VMEM((stack * width, out_width), jnp.bfloat16),
            pltpu.VMEM((2, prefix, sum_width), jnp.float32),
            pltpu.VMEM((prefix, sum_width), jnp.bfloat16),
            pltpu.SemaphoreType.DMA((SUMS + len(proj_pieces) + 2 * len(out_pieces),)),
        ],
        compiler_params=room(20),
        name="expert_steps",
    )(
        lengths,
        *dense,
        *near_memory(sums),
        *near_memory(proj_pieces),
        *near_memory(out_pieces),
    )


def shards(
    prefix_hidden,
    prefix_lengths,
    action_noise,
    prefix_gain,
    key_weight,
    value_weight,
    input_weight,
    expert_gain,
    expert_query,
    expert_key,
    expert_value,
    expert_output,
    final_gain,
    output_weight,
    *,
    group_count,
    wide_count,
):
    chips = wide_count // 2
    columns = chips // 2
    _, _, _, twin = places()
    ring = [(w, (w + 4) % wide_count) for w in range(wide_count)]
    across = [(w, w ^ 2) for w in range(wide_count)]
    beside = [(w, w ^ 1) for w in range(wide_count)]
    facing = [(g, g ^ 1) for g in range(group_count)]
    corner = [
        (g * wide_count + w, (g ^ 1) * wide_count + (w ^ 1))
        for g in range(group_count)
        for w in range(wide_count)
    ]

    def round_ring(piece):
        slots = [piece]
        for _ in range(1, columns):
            slots.append(lax.ppermute(slots[-1], "wide", ring))
        return slots

    def over(slots):
        return [lax.ppermute(slot, "wide", across) for slot in slots]

    def swap(pieces):
        return [lax.ppermute(piece, "wide", beside) for piece in pieces]

    hidden = prefix_hidden[0]
    to_corner = pick(hidden, 3, chips)
    from_corner = lax.ppermute(to_corner, ("groups", "wide"), corner)
    to_twin = pick(hidden, 1, chips)
    from_twin = lax.ppermute(to_twin, "groups", facing)
    to_core = pick(hidden, 2, chips)
    from_core = lax.ppermute(to_core, "wide", beside)
    kept, row_scale = own_part_and_scale(hidden, chips)

    half = key_weight.shape[0] // 2
    place = lax.axis_index("wide")
    gain = lax.dynamic_slice_in_dim(prefix_gain, (place * 2 + twin) * half, half, 0)

    def scaled(weight):
        part = lax.dynamic_slice_in_dim(weight, twin * half, half, 0)
        return (part.astype(jnp.float32) * gain[:, None]).astype(jnp.bfloat16)

    key_slots = round_ring(scaled(key_weight))
    value_slots = round_ring(scaled(value_weight))
    key_pieces = key_slots + over(key_slots)
    value_pieces = value_slots + over(value_slots)

    proj_own = jnp.concatenate([expert_query, expert_key, expert_value], 1)
    span = action_noise.shape[1]
    rows = -(-span // 16) * 16
    positions = jnp.concatenate(
        [
            prefix_lengths[0].astype(jnp.float32) + jnp.arange(rows, dtype=jnp.float32),
            jnp.arange(hidden.shape[0], dtype=jnp.float32),
        ]
    )
    tables = (time_embeddings(input_weight.shape[1]), *rope_tables(positions))
    proj_own, tables = lax.optimization_barrier((proj_own, tables))

    proj_slots = round_ring(proj_own)
    proj_pieces = proj_slots + over(proj_slots)
    proj_pieces = proj_pieces + swap(proj_pieces)
    out_own = jnp.concatenate([expert_output] + over([expert_output]), 0)
    out_pieces = round_ring(out_own)
    out_pieces = out_pieces + swap(out_pieces)

    corner_part, twin_part = project(
        from_corner, from_twin, key_pieces, value_pieces, columns
    )
    core_part, own_part = project(from_core, kept, key_pieces, value_pieces, columns)
    corner_paired = lax.ppermute(corner_part, "wide", beside)
    twin_sum = (twin_part + corner_paired).astype(jnp.bfloat16)
    twinned = lax.ppermute(twin_sum, "groups", facing)
    sums = (own_part, lax.ppermute(core_part, "wide", beside), twinned)

    dense = (
        action_noise[0].T,
        input_weight,
        tables[0],
        expert_gain[None, :],
        final_gain[None, :],
        output_weight.T,
        *tables[1:],
        row_scale,
    )
    actions = expert(
        prefix_lengths,
        dense,
        sums,
        proj_pieces,
        out_pieces,
        columns,
        span,
    )
    return actions.T[None]


def solution(mesh):
    placed = (
        P(("groups", "wide"), None, None),
        P(("groups", "wide")),
        P(("groups", "wide"), None, None),
        P(),
        P("wide", None),
        P("wide", None),
        P(),
        P(),
        P("wide", None),
        P("wide", None),
        P("wide", None),
        P("wide", None),
        P(),
        P(),
    )

    def whole(*arrays):
        return shards(
            *arrays, group_count=mesh.shape["groups"], wide_count=mesh.shape["wide"]
        )

    return jax.shard_map(
        whole,
        mesh=mesh,
        in_specs=placed,
        out_specs=P(("groups", "wide"), None, None),
        check_vma=False,
    )
```

```python
import functools

import jax
import jax.numpy as jnp
from jax import lax
from jax.experimental import pallas as pl
from jax.experimental.pallas import tpu as pltpu
from jax.sharding import PartitionSpec as P


HEAD = 128
STEPS = 4

rope_base = 1000000.0
norm_eps = 1e-06


ANY = pl.BlockSpec(memory_space=pl.ANY)
SMEM = pl.BlockSpec(memory_space=pltpu.SMEM)
VMEM = pl.BlockSpec(memory_space=pltpu.VMEM)


def near_memory(pieces):
    return [pltpu.with_memory_space_constraint(piece, pltpu.VMEM) for piece in pieces]


def room(mebibytes):
    return pltpu.CompilerParams(vmem_limit_bytes=mebibytes << 20)


def rope_tables(positions):
    half_width = HEAD // 2
    lane = lax.broadcasted_iota(jnp.int32, (1, HEAD), 1)
    band = (lane % half_width).astype(jnp.float32)
    angles = positions[:, None] * rope_base ** (-band * 2.0 / HEAD)
    sign = jnp.where(lane < half_width, -1.0, 1.0)
    return jnp.cos(angles), jnp.sin(angles) * sign


def time_embeddings(embed_width):
    half_width = embed_width // 2
    lane = lax.broadcasted_iota(jnp.int32, (1, embed_width), 1)
    step = lax.broadcasted_iota(jnp.int32, (STEPS, 1), 0).astype(jnp.float32)
    fraction = (lane % half_width).astype(jnp.float32) / (half_width - 1)
    period = 0.004 * (4.0 / 0.004) ** fraction
    angles = (1.0 - step / STEPS) * (2.0 * jnp.pi) / period
    return jnp.where(lane < half_width, jnp.sin(angles), jnp.cos(angles))


def places():
    place = lax.axis_index("wide")
    core = lax.rem(place, 2)
    row = lax.rem(lax.div(place, 2), 2)
    column = lax.div(place, 4)
    twin = lax.rem(lax.axis_index("groups"), 2)
    return core, row, column, twin


def chip_spots(row, column, columns):
    ring = [lax.rem(column + (columns - s), columns) for s in range(columns)]
    return [c * 2 + row for c in ring] + [c * 2 + (1 - row) for c in ring]


def pick_kernel(hidden, out, staged, sems, *, flip, chips, width):
    core, _, _, twin = places()
    core = 1 - core if flip & 2 else core
    twin = 1 - twin if flip & 1 else twin
    part = core * 2 + twin
    inward = []
    outward = []
    for chip in range(chips):
        start = pl.multiple_of((chip * 4 + part) * width, width)
        here = pl.ds(chip * width, width)
        inward.append(
            pltpu.make_async_copy(
                hidden.at[:, pl.ds(start, width)], staged.at[:, here], sems.at[chip]
            )
        )
        outward.append(
            pltpu.make_async_copy(staged.at[:, here], out.at[:, here], sems.at[chips + chip])
        )
    for copy in inward:
        copy.start()
    for first, second in zip(inward, outward):
        first.wait()
        second.start()
    for copy in outward:
        copy.wait()


def pick(hidden, flip, chips):
    row_count, depth = hidden.shape
    width = depth // chips // 4
    if width % HEAD:
        core, _, _, twin = places()
        part = (core * 2 + twin) ^ flip
        parts = hidden.reshape(row_count, chips, 4, width)
        return lax.dynamic_index_in_dim(parts, part, 2, keepdims=False).reshape(row_count, -1)
    return pl.pallas_call(
        functools.partial(pick_kernel, flip=flip, chips=chips, width=width),
        in_specs=[ANY],
        out_specs=ANY,
        out_shape=jax.ShapeDtypeStruct((row_count, depth // 4), jnp.bfloat16),
        scratch_shapes=[
            pltpu.VMEM((row_count, depth // 4), jnp.bfloat16),
            pltpu.SemaphoreType.DMA((2 * chips,)),
        ],
        compiler_params=room(4),
        name="pick_columns",
    )(hidden)


def own_kernel(hidden, kept, row_scale, *, chips, width):
    core, _, _, twin = places()
    part = core * 2 + twin
    rows = hidden[...].astype(jnp.float32)
    row_scale[...] = lax.rsqrt(jnp.mean(rows * rows, axis=-1, keepdims=True) + norm_eps)
    for chip in range(chips):
        start = pl.multiple_of((chip * 4 + part) * width, width)
        kept[:, chip * width : (chip + 1) * width] = hidden[:, pl.ds(start, width)]


def own_part_and_scale(hidden, chips):
    row_count, depth = hidden.shape
    width = depth // chips // 4
    if width % HEAD:
        rows = hidden.astype(jnp.float32)
        scale = lax.rsqrt(jnp.mean(rows * rows, axis=-1, keepdims=True) + norm_eps)
        return pick(hidden, 0, chips), scale
    step = 64
    return pl.pallas_call(
        functools.partial(own_kernel, chips=chips, width=width),
        grid=(row_count // step,),
        in_specs=[pl.BlockSpec((step, depth), lambda i: (i, 0))],
        out_specs=[
            pl.BlockSpec((step, depth // 4), lambda i: (i, 0)),
            pl.BlockSpec((step, 1), lambda i: (i, 0)),
        ],
        out_shape=[
            jax.ShapeDtypeStruct((row_count, depth // 4), jnp.bfloat16),
            jax.ShapeDtypeStruct((row_count, 1), jnp.float32),
        ],
        compiler_params=room(8),
        name="own_part",
    )(hidden)


def project_kernel(first, second, *refs, count, width, columns):
    keys = refs[:count]
    values = refs[count : 2 * count]
    first_out, second_out, rows, weight, sems = refs[2 * count :]
    _, row, column, _ = places()
    spots = chip_spots(row, column, columns)
    half = first.shape[0]
    split = weight.shape[1] // 2
    row_copies = [
        pltpu.make_async_copy(first, rows.at[pl.ds(0, half)], sems.at[2 * count]),
        pltpu.make_async_copy(second, rows.at[pl.ds(half, half)], sems.at[2 * count + 1]),
    ]
    copies = []
    for side, pieces in enumerate((keys, values)):
        for k, piece in enumerate(pieces):
            start = pl.multiple_of(spots[k] * width, width)
            copies.append(
                pltpu.make_async_copy(
                    piece,
                    weight.at[pl.ds(start, width), pl.ds(side * split, split)],
                    sems.at[side * count + k],
                )
            )
    for copy in row_copies + copies:
        copy.start()
    for copy in row_copies:
        copy.wait()
    for side in range(2):
        for copy in copies[side * count : (side + 1) * count]:
            copy.wait()
        cut = slice(side * split, (side + 1) * split)
        for out, start in ((first_out, 0), (second_out, half)):
            out[:, cut] = jnp.dot(
                rows[start : start + half], weight[:, cut], preferred_element_type=jnp.float32
            )


def project(first, second, keys, values, columns):
    width, split = keys[0].shape
    half, depth = first.shape
    count = len(keys)
    shape = jax.ShapeDtypeStruct((half, 2 * split), jnp.float32)
    return pl.pallas_call(
        functools.partial(project_kernel, count=count, width=width, columns=columns),
        in_specs=[ANY] * 2 + [VMEM] * (2 * count),
        out_specs=[VMEM, VMEM],
        out_shape=[shape, shape],
        scratch_shapes=[
            pltpu.VMEM((2 * half, depth), jnp.bfloat16),
            pltpu.VMEM((depth, 2 * split), jnp.bfloat16),
            pltpu.SemaphoreType.DMA((2 * count + 2,)),
        ],
        compiler_params=room(14),
        name="prefix_project",
    )(first, second, *near_memory(keys), *near_memory(values))


def turn(values, cosine, sine):
    return values * cosine + pltpu.roll(values, HEAD // 2, 1) * sine


LEFT_PARTS = (0, 0, 1, 0, 1, 2)
RIGHT_PARTS = (0, 1, 0, 2, 1, 0)
LOG2_E = 1.4426950408889634


def three_parts(values):
    first = values.astype(jnp.bfloat16)
    rest = values - first.astype(jnp.float32)
    second = rest.astype(jnp.bfloat16)
    third = (rest - second.astype(jnp.float32)).astype(jnp.bfloat16)
    return first, second, third


def weight_moves(pieces, columns, places_of, targets):
    core, spots = places_of
    proj, mix = targets
    moves = []
    proj_pieces, out_pieces = pieces
    for (side, k), piece in proj_pieces.items():
        rows = piece.shape[0]
        half = 1 - core if side else core
        start = pl.multiple_of((spots[k] * 2 + half) * rows, rows)
        moves.append((piece, proj.at[pl.ds(start, rows)]))
    for (side, slot), piece in out_pieces.items():
        rows = piece.shape[0] // 2
        half = 1 - core if side else core
        for cross in range(2):
            start = pl.multiple_of((spots[cross * columns + slot] * 2 + half) * rows, rows)
            moves.append((piece.at[pl.ds(cross * rows, rows)], mix.at[pl.ds(start, rows)]))
    return moves


def cache_kernel(cosine, sine, row_scale, kept, paired, twinned, keys, values, *, rows):
    groups = keys.shape[0]
    prefix = row_scale.shape[0]
    for side, out in enumerate((keys, values)):
        for g in range(groups):
            start = (side * groups + g) * HEAD
            cut = slice(start, start + HEAD)
            raw = kept[:, cut] + paired[:, cut] + twinned[:, cut].astype(jnp.float32)
            raw = raw * row_scale[...]
            if side == 0:
                raw = turn(raw, cosine[rows:], sine[rows:])
            out[g, :prefix] = raw.astype(jnp.bfloat16)
        out[:, prefix:] = jnp.zeros_like(out[:, prefix:])


def cache(cosine, sine, row_scale, sums, rows):
    prefix, sum_width = sums[0].shape
    groups = sum_width // HEAD // 2
    total = -(-(prefix + rows) // HEAD) * HEAD
    return pl.pallas_call(
        functools.partial(cache_kernel, rows=rows),
        in_specs=[VMEM] * 6,
        out_specs=[VMEM] * 2,
        out_shape=[pltpu.VMEM((groups, total, HEAD), jnp.bfloat16)] * 2,
        compiler_params=room(4),
        name="prefix_cache",
    )(*near_memory((cosine, sine, row_scale)), *near_memory(sums))


def prepare_kernel(
    noise, input_weight, output_weight, *refs, columns, span, proj_slots, out_slots
):
    proj_pieces = dict(zip(proj_slots, refs))
    refs = refs[len(proj_slots) :]
    out_pieces = dict(zip(out_slots, refs))
    refs = refs[len(out_slots) :]
    proj, mix, input_parts, output_parts, state, turned, sems = refs
    core, row, column, _ = places()
    spots = chip_spots(row, column, columns)
    moves = weight_moves((proj_pieces, out_pieces), columns, (core, spots), (proj, mix))
    copies = [
        pltpu.make_async_copy(source, target, sems.at[k])
        for k, (source, target) in enumerate(moves)
    ]
    for copy in copies:
        copy.start()
    width = noise.shape[0]
    weight_parts = three_parts(input_weight[...])
    turned[...] = jnp.zeros_like(turned)
    for k, part in enumerate(RIGHT_PARTS):
        cut = slice(k * width, (k + 1) * width)
        input_parts[cut] = weight_parts[part]
        output_parts[cut] = output_weight[...]
        turned[cut, :span] = noise[...]
    state[...] = turned[...].T
    for copy in copies:
        copy.wait()


def prepare(dense, proj_pieces, out_pieces, proj_depth, out_depth, columns, rows, span):
    proj_width = next(iter(proj_pieces.values())).shape[1]
    out_width = next(iter(out_pieces.values())).shape[1]
    stack = len(LEFT_PARTS) * dense[0].shape[0]
    moves = len(proj_pieces) + 2 * len(out_pieces)
    shapes = [
        pltpu.VMEM((proj_depth, proj_width), jnp.bfloat16),
        pltpu.VMEM((out_depth, out_width), jnp.bfloat16),
        pltpu.VMEM((stack, out_width), jnp.bfloat16),
        pltpu.VMEM((stack, out_width), jnp.bfloat16),
        pltpu.VMEM((rows, stack), jnp.float32),
    ]
    near = near_memory([*proj_pieces.values(), *out_pieces.values()])
    return pl.pallas_call(
        functools.partial(
            prepare_kernel,
            columns=columns,
            span=span,
            proj_slots=tuple(proj_pieces),
            out_slots=tuple(out_pieces),
        ),
        in_specs=[VMEM] * (len(dense) + len(near)),
        out_specs=[VMEM] * len(shapes),
        out_shape=shapes,
        scratch_shapes=[
            pltpu.VMEM((stack, rows), jnp.float32),
            pltpu.SemaphoreType.DMA((moves,)),
        ],
        compiler_params=room(8),
        name="expert_prepare",
    )(*dense, *near)


def expert_kernel(
    lengths,
    embed,
    expert_gain,
    final_gain,
    cosine,
    sine,
    first_proj,
    first_mix,
    first_keys,
    first_values,
    input_parts,
    output_parts,
    first_state,
    *refs,
    columns,
    prefix,
    width,
    span,
    proj_slots,
    out_slots,
):
    proj_pieces = dict(zip(proj_slots, refs))
    refs = refs[len(proj_slots) :]
    out_pieces = dict(zip(out_slots, refs))
    actions, proj, mix, keys, values, joined, score_ref, chance_ref, state_ref, turned, sems = refs[
        len(out_slots) :
    ]
    core, row, column, _ = places()
    spots = chip_spots(row, column, columns)
    moves = weight_moves((proj_pieces, out_pieces), columns, (core, spots), (proj, mix))
    copies = [
        pltpu.make_async_copy(source, target, sems.at[k])
        for k, (source, target) in enumerate(moves)
    ]
    for copy in copies:
        copy.start()
    early, late = copies[: len(proj_slots)], copies[len(proj_slots) :]
    groups = keys.shape[0]
    rows, wide = first_state.shape
    heads = joined.shape[1] // HEAD
    state_ref[...] = first_state[...]
    action_cos = cosine[:rows]
    action_sin = sine[:rows]
    query_cos = action_cos * (HEAD ** (-0.5) * LOG2_E)
    query_sin = action_sin * (HEAD ** (-0.5) * LOG2_E)

    ratio = heads // groups
    query_width = heads * HEAD
    kv_width = groups * HEAD
    contract = (((1,), (1,)), ((), ()))
    place = lax.broadcasted_iota(jnp.int32, (1, keys.shape[1]), 1)
    allowed = (place < lengths[0]) | ((place >= prefix) & (place < prefix + span))
    lane = lax.broadcasted_iota(jnp.int32, (1, wide), 1)
    is_second = (lane < 0)
    is_third = is_second
    for k, part in enumerate(LEFT_PARTS):
        here = (lane >= k * width) & (lane < (k + 1) * width)
        if part == 1:
            is_second = is_second | here
        if part == 2:
            is_third = is_third | here

    def step(k, carry):
        state = state_ref[...]
        first = state.astype(jnp.bfloat16).astype(jnp.float32)
        rest_part = state - first
        second = rest_part.astype(jnp.bfloat16).astype(jnp.float32)
        third = rest_part - second
        parts = jnp.where(is_third, third, jnp.where(is_second, second, first))
        hidden = jnp.dot(
            parts.astype(jnp.bfloat16), input_parts[...], preferred_element_type=jnp.float32
        )
        hidden = hidden + embed[pl.ds(k, 1), :]
        square = jnp.mean(hidden * hidden, axis=-1, keepdims=True)
        normed = (hidden * lax.rsqrt(square + norm_eps) * expert_gain[...]).astype(jnp.bfloat16)

        @pl.when(k == 0)
        def _():
            for copy in early:
                copy.wait()

        raw = jnp.dot(normed, proj[...], preferred_element_type=jnp.float32)

        @pl.when(k == 0)
        def _():
            for copy in late:
                copy.wait()

        base = query_width + kv_width
        for g in range(groups):
            keys[g, prefix : prefix + rows] = turn(
                raw[:, query_width + g * HEAD : query_width + (g + 1) * HEAD],
                action_cos,
                action_sin,
            ).astype(jnp.bfloat16)
            values[g, prefix : prefix + rows] = raw[
                :, base + g * HEAD : base + (g + 1) * HEAD
            ].astype(jnp.bfloat16)
            queries = jnp.concatenate(
                [
                    turn(
                        raw[:, (g * ratio + r) * HEAD : (g * ratio + r + 1) * HEAD],
                        query_cos,
                        query_sin,
                    ).astype(jnp.bfloat16)
                    for r in range(ratio)
                ],
                0,
            )
            cut = slice(g * ratio * rows, (g + 1) * ratio * rows)
            score_ref[cut] = lax.dot_general(
                queries, keys[g], contract, preferred_element_type=jnp.float32
            )
        scores = jnp.where(allowed, score_ref[...], -1e30)
        scores = jnp.exp2(scores - jnp.max(scores, -1, keepdims=True))
        inverse = 1.0 / jnp.sum(scores, -1, keepdims=True)
        chance_ref[...] = scores.astype(jnp.bfloat16)
        for g in range(groups):
            cut = slice(g * ratio * rows, (g + 1) * ratio * rows)
            mixed = jnp.dot(chance_ref[cut], values[g], preferred_element_type=jnp.float32)
            mixed = (mixed * inverse[cut]).astype(jnp.bfloat16)
            for r in range(ratio):
                h = g * ratio + r
                joined[:, h * HEAD : (h + 1) * HEAD] = mixed[r * rows : (r + 1) * rows]
        hidden = hidden + jnp.dot(joined[...], mix[...], preferred_element_type=jnp.float32)
        square = jnp.mean(hidden * hidden, axis=-1, keepdims=True)
        normed = (hidden * lax.rsqrt(square + norm_eps) * final_gain[...]).astype(jnp.bfloat16)
        velocity = lax.dot_general(
            normed, output_parts[...], contract, preferred_element_type=jnp.float32
        )
        state_ref[...] = state - velocity / STEPS
        return carry

    lax.fori_loop(0, STEPS, step, 0)
    turned[...] = state_ref[...].T
    actions[...] = turned[:width, :span]


def expert(lengths, dense, prepared, proj_pieces, out_pieces, columns, prefix, width, span):
    depth, _ = prepared[1].shape
    rows = prepared[6].shape[0]
    heads = depth // HEAD
    pieces = near_memory([*proj_pieces.values(), *out_pieces.values()])
    first = 1 + len(dense)
    shapes = [jax.ShapeDtypeStruct((width, span), jnp.float32)]
    shapes += [pltpu.VMEM(v.shape, v.dtype) for v in prepared[:4]]
    return pl.pallas_call(
        functools.partial(
            expert_kernel,
            columns=columns,
            prefix=prefix,
            width=width,
            span=span,
            proj_slots=tuple(proj_pieces),
            out_slots=tuple(out_pieces),
        ),
        in_specs=[SMEM] + [VMEM] * (len(dense) + len(prepared) + len(pieces)),
        out_specs=[VMEM] * len(shapes),
        out_shape=shapes,
        input_output_aliases={first + k: 1 + k for k in range(4)},
        scratch_shapes=[
            pltpu.VMEM((rows, heads * HEAD), jnp.bfloat16),
            pltpu.VMEM((rows * heads, prepared[2].shape[1]), jnp.float32),
            pltpu.VMEM((rows * heads, prepared[2].shape[1]), jnp.bfloat16),
            pltpu.VMEM(prepared[6].shape, jnp.float32),
            pltpu.VMEM(prepared[6].shape[::-1], jnp.float32),
            pltpu.SemaphoreType.DMA((len(proj_pieces) + 2 * len(out_pieces),)),
        ],
        compiler_params=room(8),
        name="expert_steps",
    )(lengths, *dense, *prepared, *pieces)[0]


def shards(
    prefix_hidden,
    prefix_lengths,
    action_noise,
    prefix_gain,
    key_weight,
    value_weight,
    input_weight,
    expert_gain,
    expert_query,
    expert_key,
    expert_value,
    expert_output,
    final_gain,
    output_weight,
    *,
    group_count,
    wide_count,
):
    chips = wide_count // 2
    columns = chips // 2
    _, _, _, twin = places()
    ring = [(w, (w + 4) % wide_count) for w in range(wide_count)]
    across = [(w, w ^ 2) for w in range(wide_count)]
    beside = [(w, w ^ 1) for w in range(wide_count)]
    facing = [(g, g ^ 1) for g in range(group_count)]
    corner = [
        (g * wide_count + w, (g ^ 1) * wide_count + (w ^ 1))
        for g in range(group_count)
        for w in range(wide_count)
    ]

    def round_ring(piece):
        slots = [piece]
        for _ in range(1, columns):
            slots.append(lax.ppermute(slots[-1], "wide", ring))
        return slots

    def over(slots):
        return [lax.ppermute(slot, "wide", across) for slot in slots]

    def swap(pieces):
        return [lax.ppermute(piece, "wide", beside) for piece in pieces]

    hidden = prefix_hidden[0]
    to_corner = pick(hidden, 3, chips)
    from_corner = lax.ppermute(to_corner, ("groups", "wide"), corner)
    to_twin = pick(hidden, 1, chips)
    from_twin = lax.ppermute(to_twin, "groups", facing)
    to_core = pick(hidden, 2, chips)
    from_core = lax.ppermute(to_core, "wide", beside)
    kept, row_scale = own_part_and_scale(hidden, chips)

    half = key_weight.shape[0] // 2
    place = lax.axis_index("wide")
    gain = lax.dynamic_slice_in_dim(prefix_gain, (place * 2 + twin) * half, half, 0)

    def scaled(weight):
        part = lax.dynamic_slice_in_dim(weight, twin * half, half, 0)
        return (part.astype(jnp.float32) * gain[:, None]).astype(jnp.bfloat16)

    key_slots = round_ring(scaled(key_weight))
    value_slots = round_ring(scaled(value_weight))
    key_pieces = key_slots + over(key_slots)
    value_pieces = value_slots + over(value_slots)

    proj_own = jnp.concatenate([expert_query, expert_key, expert_value], 1)
    span = action_noise.shape[1]
    rows = -(-span // 16) * 16
    positions = jnp.concatenate(
        [
            prefix_lengths[0].astype(jnp.float32) + jnp.arange(rows, dtype=jnp.float32),
            jnp.arange(hidden.shape[0], dtype=jnp.float32),
        ]
    )
    tables = (time_embeddings(input_weight.shape[1]), *rope_tables(positions))
    proj_own, tables = lax.optimization_barrier((proj_own, tables))

    proj_slots = round_ring(proj_own)
    proj_pieces = proj_slots + over(proj_slots)
    proj_pieces = proj_pieces + swap(proj_pieces)
    out_own = jnp.concatenate([expert_output] + over([expert_output]), 0)
    out_pieces = round_ring(out_own)
    out_pieces = out_pieces + swap(out_pieces)

    corner_part, twin_part = project(
        from_corner, from_twin, key_pieces, value_pieces, columns
    )
    core_part, own_part = project(from_core, kept, key_pieces, value_pieces, columns)
    corner_paired = lax.ppermute(corner_part, "wide", beside)
    twin_sum = (twin_part + corner_paired).astype(jnp.bfloat16)
    twinned = lax.ppermute(twin_sum, "groups", facing)
    sums = (own_part, lax.ppermute(core_part, "wide", beside), twinned)

    span, width = action_noise.shape[1:]
    last = columns - 1
    proj_all = {
        (k // (2 * columns), k % (2 * columns)): piece for k, piece in enumerate(proj_pieces)
    }
    out_all = {(k // columns, k % columns): piece for k, piece in enumerate(out_pieces)}
    split = lambda pieces, ends: {
        key: piece for key, piece in pieces.items() if (key[1] % columns == last) == ends
    }
    prefix_tables = tables[1:]
    prefix_keys, prefix_values = cache(*prefix_tables, row_scale, sums, rows)
    proj, mix, *constants = prepare(
        (action_noise[0].T, input_weight, output_weight.T),
        split(proj_all, False),
        split(out_all, False),
        proj_own.shape[0] * wide_count,
        expert_output.shape[0] * wide_count,
        columns,
        rows,
        span,
    )
    actions = expert(
        prefix_lengths,
        (tables[0], expert_gain[None, :], final_gain[None, :], *prefix_tables),
        (proj, mix, prefix_keys, prefix_values, *constants),
        split(proj_all, True),
        split(out_all, True),
        columns,
        hidden.shape[0],
        width,
        span,
    )
    return actions.T[None]


def solution(mesh):
    placed = (
        P(("groups", "wide"), None, None),
        P(("groups", "wide")),
        P(("groups", "wide"), None, None),
        P(),
        P("wide", None),
        P("wide", None),
        P(),
        P(),
        P("wide", None),
        P("wide", None),
        P("wide", None),
        P("wide", None),
        P(),
        P(),
    )

    def whole(*arrays):
        return shards(
            *arrays, group_count=mesh.shape["groups"], wide_count=mesh.shape["wide"]
        )

    return jax.shard_map(
        whole,
        mesh=mesh,
        in_specs=placed,
        out_specs=P(("groups", "wide"), None, None),
        check_vma=False,
    )
```

```python
import functools

import jax
import jax.numpy as jnp
from jax import lax
from jax.experimental import pallas as pl
from jax.experimental.pallas import tpu as pltpu
from jax.sharding import PartitionSpec as P


HEAD = 128
STEPS = 4

rope_base = 1000000.0
norm_eps = 1e-06


ANY = pl.BlockSpec(memory_space=pl.ANY)
SMEM = pl.BlockSpec(memory_space=pltpu.SMEM)
VMEM = pl.BlockSpec(memory_space=pltpu.VMEM)


def near_memory(pieces):
    return [pltpu.with_memory_space_constraint(piece, pltpu.VMEM) for piece in pieces]


def room(mebibytes):
    return pltpu.CompilerParams(vmem_limit_bytes=mebibytes << 20)


def rope_tables(positions):
    half_width = HEAD // 2
    lane = lax.broadcasted_iota(jnp.int32, (1, HEAD), 1)
    band = (lane % half_width).astype(jnp.float32)
    angles = positions[:, None] * rope_base ** (-band * 2.0 / HEAD)
    sign = jnp.where(lane < half_width, -1.0, 1.0)
    return jnp.cos(angles), jnp.sin(angles) * sign


def time_embeddings(embed_width):
    half_width = embed_width // 2
    lane = lax.broadcasted_iota(jnp.int32, (1, embed_width), 1)
    step = lax.broadcasted_iota(jnp.int32, (STEPS, 1), 0).astype(jnp.float32)
    fraction = (lane % half_width).astype(jnp.float32) / (half_width - 1)
    period = 0.004 * (4.0 / 0.004) ** fraction
    angles = (1.0 - step / STEPS) * (2.0 * jnp.pi) / period
    return jnp.where(lane < half_width, jnp.sin(angles), jnp.cos(angles))


def places():
    place = lax.axis_index("wide")
    core = lax.rem(place, 2)
    row = lax.rem(lax.div(place, 2), 2)
    column = lax.div(place, 4)
    twin = lax.rem(lax.axis_index("groups"), 2)
    return core, row, column, twin


def chip_spots(row, column, columns):
    ring = [lax.rem(column + (columns - s), columns) for s in range(columns)]
    return [c * 2 + row for c in ring] + [c * 2 + (1 - row) for c in ring]


def pick_kernel(hidden, out, staged, sems, *, flip, chips, width):
    core, _, _, twin = places()
    core = 1 - core if flip & 2 else core
    twin = 1 - twin if flip & 1 else twin
    part = core * 2 + twin
    inward = []
    outward = []
    for chip in range(chips):
        start = pl.multiple_of((chip * 4 + part) * width, width)
        here = pl.ds(chip * width, width)
        inward.append(
            pltpu.make_async_copy(
                hidden.at[:, pl.ds(start, width)], staged.at[:, here], sems.at[chip]
            )
        )
        outward.append(
            pltpu.make_async_copy(staged.at[:, here], out.at[:, here], sems.at[chips + chip])
        )
    for copy in inward:
        copy.start()
    for first, second in zip(inward, outward):
        first.wait()
        second.start()
    for copy in outward:
        copy.wait()


def pick(hidden, flip, chips):
    row_count, depth = hidden.shape
    width = depth // chips // 4
    if width % HEAD:
        core, _, _, twin = places()
        part = (core * 2 + twin) ^ flip
        parts = hidden.reshape(row_count, chips, 4, width)
        return lax.dynamic_index_in_dim(parts, part, 2, keepdims=False).reshape(row_count, -1)
    return pl.pallas_call(
        functools.partial(pick_kernel, flip=flip, chips=chips, width=width),
        in_specs=[ANY],
        out_specs=ANY,
        out_shape=jax.ShapeDtypeStruct((row_count, depth // 4), jnp.bfloat16),
        scratch_shapes=[
            pltpu.VMEM((row_count, depth // 4), jnp.bfloat16),
            pltpu.SemaphoreType.DMA((2 * chips,)),
        ],
        compiler_params=room(4),
        name="pick_columns",
    )(hidden)


def own_kernel(hidden, kept, row_scale, *, chips, width):
    core, _, _, twin = places()
    part = core * 2 + twin
    rows = hidden[...].astype(jnp.float32)
    row_scale[...] = lax.rsqrt(jnp.mean(rows * rows, axis=-1, keepdims=True) + norm_eps)
    for chip in range(chips):
        start = pl.multiple_of((chip * 4 + part) * width, width)
        kept[:, chip * width : (chip + 1) * width] = hidden[:, pl.ds(start, width)]


def own_part_and_scale(hidden, chips):
    row_count, depth = hidden.shape
    width = depth // chips // 4
    if width % HEAD:
        rows = hidden.astype(jnp.float32)
        scale = lax.rsqrt(jnp.mean(rows * rows, axis=-1, keepdims=True) + norm_eps)
        return pick(hidden, 0, chips), scale
    step = 64
    return pl.pallas_call(
        functools.partial(own_kernel, chips=chips, width=width),
        grid=(row_count // step,),
        in_specs=[pl.BlockSpec((step, depth), lambda i: (i, 0))],
        out_specs=[
            pl.BlockSpec((step, depth // 4), lambda i: (i, 0)),
            pl.BlockSpec((step, 1), lambda i: (i, 0)),
        ],
        out_shape=[
            jax.ShapeDtypeStruct((row_count, depth // 4), jnp.bfloat16),
            jax.ShapeDtypeStruct((row_count, 1), jnp.float32),
        ],
        compiler_params=room(8),
        name="own_part",
    )(hidden)


def project_kernel(first, second, *refs, count, width, columns):
    keys = refs[:count]
    values = refs[count : 2 * count]
    first_out, second_out, rows, weight, sems = refs[2 * count :]
    _, row, column, _ = places()
    spots = chip_spots(row, column, columns)
    half = first.shape[0]
    split = weight.shape[1] // 2
    row_copies = [
        pltpu.make_async_copy(first, rows.at[pl.ds(0, half)], sems.at[2 * count]),
        pltpu.make_async_copy(second, rows.at[pl.ds(half, half)], sems.at[2 * count + 1]),
    ]
    copies = []
    for side, pieces in enumerate((keys, values)):
        for k, piece in enumerate(pieces):
            start = pl.multiple_of(spots[k] * width, width)
            copies.append(
                pltpu.make_async_copy(
                    piece,
                    weight.at[pl.ds(start, width), pl.ds(side * split, split)],
                    sems.at[side * count + k],
                )
            )
    for copy in row_copies + copies:
        copy.start()
    for copy in row_copies:
        copy.wait()
    for side in range(2):
        for copy in copies[side * count : (side + 1) * count]:
            copy.wait()
        cut = slice(side * split, (side + 1) * split)
        for out, start in ((first_out, 0), (second_out, half)):
            out[:, cut] = jnp.dot(
                rows[start : start + half], weight[:, cut], preferred_element_type=jnp.float32
            )


def project(first, second, keys, values, columns):
    width, split = keys[0].shape
    half, depth = first.shape
    count = len(keys)
    shape = jax.ShapeDtypeStruct((half, 2 * split), jnp.float32)
    return pl.pallas_call(
        functools.partial(project_kernel, count=count, width=width, columns=columns),
        in_specs=[ANY] * 2 + [VMEM] * (2 * count),
        out_specs=[VMEM, VMEM],
        out_shape=[shape, shape],
        scratch_shapes=[
            pltpu.VMEM((2 * half, depth), jnp.bfloat16),
            pltpu.VMEM((depth, 2 * split), jnp.bfloat16),
            pltpu.SemaphoreType.DMA((2 * count + 2,)),
        ],
        compiler_params=room(14),
        name="prefix_project",
    )(first, second, *near_memory(keys), *near_memory(values))


def turn(values, cosine, sine):
    return values * cosine + pltpu.roll(values, HEAD // 2, 1) * sine


LEFT_PARTS = (0, 0, 1, 0, 1, 2)
RIGHT_PARTS = (0, 1, 0, 2, 1, 0)
LOG2_E = 1.4426950408889634


def three_parts(values):
    first = values.astype(jnp.bfloat16)
    rest = values - first.astype(jnp.float32)
    second = rest.astype(jnp.bfloat16)
    third = (rest - second.astype(jnp.float32)).astype(jnp.bfloat16)
    return first, second, third


def weight_moves(pieces, columns, places_of, targets):
    core, spots = places_of
    proj, mix = targets
    moves = []
    proj_pieces, out_pieces = pieces
    for (side, k), piece in proj_pieces.items():
        rows = piece.shape[0]
        half = 1 - core if side else core
        start = pl.multiple_of((spots[k] * 2 + half) * rows, rows)
        moves.append((piece, proj.at[pl.ds(start, rows)]))
    for (side, slot), piece in out_pieces.items():
        rows = piece.shape[0] // 2
        half = 1 - core if side else core
        for cross in range(2):
            start = pl.multiple_of((spots[cross * columns + slot] * 2 + half) * rows, rows)
            moves.append((piece.at[pl.ds(cross * rows, rows)], mix.at[pl.ds(start, rows)]))
    return moves


def cache_kernel(cosine, sine, row_scale, kept, paired, twinned, keys, values, *, rows):
    groups = keys.shape[0]
    prefix = row_scale.shape[0]
    for side, out in enumerate((keys, values)):
        for g in range(groups):
            start = (side * groups + g) * HEAD
            cut = slice(start, start + HEAD)
            raw = kept[:, cut] + paired[:, cut] + twinned[:, cut].astype(jnp.float32)
            raw = raw * row_scale[...]
            if side == 0:
                raw = turn(raw, cosine[rows:], sine[rows:])
            out[g, :prefix] = raw.astype(jnp.bfloat16)
        out[:, prefix:] = jnp.zeros_like(out[:, prefix:])


def cache(cosine, sine, row_scale, sums, rows):
    prefix, sum_width = sums[0].shape
    groups = sum_width // HEAD // 2
    total = -(-(prefix + rows) // HEAD) * HEAD
    return pl.pallas_call(
        functools.partial(cache_kernel, rows=rows),
        in_specs=[VMEM] * 6,
        out_specs=[VMEM] * 2,
        out_shape=[pltpu.VMEM((groups, total, HEAD), jnp.bfloat16)] * 2,
        compiler_params=room(4),
        name="prefix_cache",
    )(*near_memory((cosine, sine, row_scale)), *near_memory(sums))


def prepare_kernel(
    noise, input_weight, output_weight, *refs, columns, span, proj_slots, out_slots
):
    proj_pieces = dict(zip(proj_slots, refs))
    refs = refs[len(proj_slots) :]
    out_pieces = dict(zip(out_slots, refs))
    refs = refs[len(out_slots) :]
    proj, mix, input_parts, output_parts, state, turned, sems = refs
    core, row, column, _ = places()
    spots = chip_spots(row, column, columns)
    moves = weight_moves((proj_pieces, out_pieces), columns, (core, spots), (proj, mix))
    copies = [
        pltpu.make_async_copy(source, target, sems.at[k])
        for k, (source, target) in enumerate(moves)
    ]
    for copy in copies:
        copy.start()
    width = noise.shape[0]
    weight_parts = three_parts(input_weight[...])
    turned[...] = jnp.zeros_like(turned)
    for k, part in enumerate(RIGHT_PARTS):
        cut = slice(k * width, (k + 1) * width)
        input_parts[cut] = weight_parts[part]
        output_parts[cut] = output_weight[...]
        turned[cut, :span] = noise[...]
    state[...] = turned[...].T
    for copy in copies:
        copy.wait()


def prepare(dense, proj_pieces, out_pieces, proj_depth, out_depth, columns, rows, span):
    proj_width = next(iter(proj_pieces.values())).shape[1]
    out_width = next(iter(out_pieces.values())).shape[1]
    stack = len(LEFT_PARTS) * dense[0].shape[0]
    moves = len(proj_pieces) + 2 * len(out_pieces)
    shapes = [
        pltpu.VMEM((proj_depth, proj_width), jnp.bfloat16),
        pltpu.VMEM((out_depth, out_width), jnp.bfloat16),
        pltpu.VMEM((stack, out_width), jnp.bfloat16),
        pltpu.VMEM((stack, out_width), jnp.bfloat16),
        pltpu.VMEM((rows, stack), jnp.float32),
    ]
    near = near_memory([*proj_pieces.values(), *out_pieces.values()])
    return pl.pallas_call(
        functools.partial(
            prepare_kernel,
            columns=columns,
            span=span,
            proj_slots=tuple(proj_pieces),
            out_slots=tuple(out_pieces),
        ),
        in_specs=[VMEM] * (len(dense) + len(near)),
        out_specs=[VMEM] * len(shapes),
        out_shape=shapes,
        scratch_shapes=[
            pltpu.VMEM((stack, rows), jnp.float32),
            pltpu.SemaphoreType.DMA((moves,)),
        ],
        compiler_params=room(8),
        name="expert_prepare",
    )(*dense, *near)


def expert_kernel(
    lengths,
    embed,
    expert_gain,
    final_gain,
    cosine,
    sine,
    first_proj,
    first_mix,
    first_keys,
    first_values,
    input_parts,
    output_parts,
    first_state,
    *refs,
    columns,
    prefix,
    width,
    span,
    proj_slots,
    out_slots,
):
    proj_pieces = dict(zip(proj_slots, refs))
    refs = refs[len(proj_slots) :]
    out_pieces = dict(zip(out_slots, refs))
    actions, proj, mix, keys, values, joined, score_ref, chance_ref, state_ref, turned, sems = refs[
        len(out_slots) :
    ]
    core, row, column, _ = places()
    spots = chip_spots(row, column, columns)
    moves = weight_moves((proj_pieces, out_pieces), columns, (core, spots), (proj, mix))
    copies = [
        pltpu.make_async_copy(source, target, sems.at[k])
        for k, (source, target) in enumerate(moves)
    ]
    for copy in copies:
        copy.start()
    early, late = copies[: len(proj_slots)], copies[len(proj_slots) :]
    groups = keys.shape[0]
    rows, wide = first_state.shape
    heads = joined.shape[1] // HEAD
    state_ref[...] = first_state[...]
    action_cos = cosine[:rows]
    action_sin = sine[:rows]
    query_cos = action_cos * (HEAD ** (-0.5) * LOG2_E)
    query_sin = action_sin * (HEAD ** (-0.5) * LOG2_E)

    ratio = heads // groups
    query_width = heads * HEAD
    kv_width = groups * HEAD
    contract = (((1,), (1,)), ((), ()))
    place = lax.broadcasted_iota(jnp.int32, (1, keys.shape[1]), 1)
    allowed = (place < lengths[0]) | ((place >= prefix) & (place < prefix + span))
    lane = lax.broadcasted_iota(jnp.int32, (1, wide), 1)
    is_second = (lane < 0)
    is_third = is_second
    for k, part in enumerate(LEFT_PARTS):
        here = (lane >= k * width) & (lane < (k + 1) * width)
        if part == 1:
            is_second = is_second | here
        if part == 2:
            is_third = is_third | here

    def step(k):
        state = state_ref[...]
        first = state.astype(jnp.bfloat16).astype(jnp.float32)
        rest_part = state - first
        second = rest_part.astype(jnp.bfloat16).astype(jnp.float32)
        third = rest_part - second
        parts = jnp.where(is_third, third, jnp.where(is_second, second, first))
        hidden = jnp.dot(
            parts.astype(jnp.bfloat16), input_parts[...], preferred_element_type=jnp.float32
        )
        hidden = hidden + embed[k : k + 1, :]
        square = jnp.mean(hidden * hidden, axis=-1, keepdims=True)
        normed = (hidden * lax.rsqrt(square + norm_eps) * expert_gain[...]).astype(jnp.bfloat16)

        if k == 0:
            for copy in early:
                copy.wait()

        raw = jnp.dot(normed, proj[...], preferred_element_type=jnp.float32)

        if k == 0:
            for copy in late:
                copy.wait()

        base = query_width + kv_width
        for g in range(groups):
            keys[g, prefix : prefix + rows] = turn(
                raw[:, query_width + g * HEAD : query_width + (g + 1) * HEAD],
                action_cos,
                action_sin,
            ).astype(jnp.bfloat16)
            values[g, prefix : prefix + rows] = raw[
                :, base + g * HEAD : base + (g + 1) * HEAD
            ].astype(jnp.bfloat16)
            queries = jnp.concatenate(
                [
                    turn(
                        raw[:, (g * ratio + r) * HEAD : (g * ratio + r + 1) * HEAD],
                        query_cos,
                        query_sin,
                    ).astype(jnp.bfloat16)
                    for r in range(ratio)
                ],
                0,
            )
            cut = slice(g * ratio * rows, (g + 1) * ratio * rows)
            score_ref[cut] = lax.dot_general(
                queries, keys[g], contract, preferred_element_type=jnp.float32
            )
        scores = jnp.where(allowed, score_ref[...], -1e30)
        scores = jnp.exp2(scores - jnp.max(scores, -1, keepdims=True))
        inverse = 1.0 / jnp.sum(scores, -1, keepdims=True)
        chance_ref[...] = scores.astype(jnp.bfloat16)
        for g in range(groups):
            cut = slice(g * ratio * rows, (g + 1) * ratio * rows)
            mixed = jnp.dot(chance_ref[cut], values[g], preferred_element_type=jnp.float32)
            mixed = (mixed * inverse[cut]).astype(jnp.bfloat16)
            for r in range(ratio):
                h = g * ratio + r
                joined[:, h * HEAD : (h + 1) * HEAD] = mixed[r * rows : (r + 1) * rows]
        hidden = hidden + jnp.dot(joined[...], mix[...], preferred_element_type=jnp.float32)
        square = jnp.mean(hidden * hidden, axis=-1, keepdims=True)
        normed = (hidden * lax.rsqrt(square + norm_eps) * final_gain[...]).astype(jnp.bfloat16)
        velocity = lax.dot_general(
            normed, output_parts[...], contract, preferred_element_type=jnp.float32
        )
        state_ref[...] = state - velocity / STEPS

    for k in range(STEPS):
        step(k)
    turned[...] = state_ref[...].T
    actions[...] = turned[:width, :span]


def expert(lengths, dense, prepared, proj_pieces, out_pieces, columns, prefix, width, span):
    depth, _ = prepared[1].shape
    rows = prepared[6].shape[0]
    heads = depth // HEAD
    pieces = near_memory([*proj_pieces.values(), *out_pieces.values()])
    first = 1 + len(dense)
    shapes = [jax.ShapeDtypeStruct((width, span), jnp.float32)]
    shapes += [pltpu.VMEM(v.shape, v.dtype) for v in prepared[:4]]
    return pl.pallas_call(
        functools.partial(
            expert_kernel,
            columns=columns,
            prefix=prefix,
            width=width,
            span=span,
            proj_slots=tuple(proj_pieces),
            out_slots=tuple(out_pieces),
        ),
        in_specs=[SMEM] + [VMEM] * (len(dense) + len(prepared) + len(pieces)),
        out_specs=[VMEM] * len(shapes),
        out_shape=shapes,
        input_output_aliases={first + k: 1 + k for k in range(4)},
        scratch_shapes=[
            pltpu.VMEM((rows, heads * HEAD), jnp.bfloat16),
            pltpu.VMEM((rows * heads, prepared[2].shape[1]), jnp.float32),
            pltpu.VMEM((rows * heads, prepared[2].shape[1]), jnp.bfloat16),
            pltpu.VMEM(prepared[6].shape, jnp.float32),
            pltpu.VMEM(prepared[6].shape[::-1], jnp.float32),
            pltpu.SemaphoreType.DMA((len(proj_pieces) + 2 * len(out_pieces),)),
        ],
        compiler_params=room(8),
        name="expert_steps",
    )(lengths, *dense, *prepared, *pieces)[0]


def shards(
    prefix_hidden,
    prefix_lengths,
    action_noise,
    prefix_gain,
    key_weight,
    value_weight,
    input_weight,
    expert_gain,
    expert_query,
    expert_key,
    expert_value,
    expert_output,
    final_gain,
    output_weight,
    *,
    group_count,
    wide_count,
):
    chips = wide_count // 2
    columns = chips // 2
    _, _, _, twin = places()
    ring = [(w, (w + 4) % wide_count) for w in range(wide_count)]
    across = [(w, w ^ 2) for w in range(wide_count)]
    beside = [(w, w ^ 1) for w in range(wide_count)]
    facing = [(g, g ^ 1) for g in range(group_count)]
    corner = [
        (g * wide_count + w, (g ^ 1) * wide_count + (w ^ 1))
        for g in range(group_count)
        for w in range(wide_count)
    ]

    def round_ring(piece):
        slots = [piece]
        for _ in range(1, columns):
            slots.append(lax.ppermute(slots[-1], "wide", ring))
        return slots

    def over(slots):
        return [lax.ppermute(slot, "wide", across) for slot in slots]

    def swap(pieces):
        return [lax.ppermute(piece, "wide", beside) for piece in pieces]

    hidden = prefix_hidden[0]
    to_corner = pick(hidden, 3, chips)
    from_corner = lax.ppermute(to_corner, ("groups", "wide"), corner)
    to_twin = pick(hidden, 1, chips)
    from_twin = lax.ppermute(to_twin, "groups", facing)
    to_core = pick(hidden, 2, chips)
    from_core = lax.ppermute(to_core, "wide", beside)
    kept, row_scale = own_part_and_scale(hidden, chips)

    half = key_weight.shape[0] // 2
    place = lax.axis_index("wide")
    gain = lax.dynamic_slice_in_dim(prefix_gain, (place * 2 + twin) * half, half, 0)

    def scaled(weight):
        part = lax.dynamic_slice_in_dim(weight, twin * half, half, 0)
        return (part.astype(jnp.float32) * gain[:, None]).astype(jnp.bfloat16)

    key_slots = round_ring(scaled(key_weight))
    value_slots = round_ring(scaled(value_weight))
    key_pieces = key_slots + over(key_slots)
    value_pieces = value_slots + over(value_slots)

    proj_own = jnp.concatenate([expert_query, expert_key, expert_value], 1)
    span = action_noise.shape[1]
    rows = -(-span // 16) * 16
    positions = jnp.concatenate(
        [
            prefix_lengths[0].astype(jnp.float32) + jnp.arange(rows, dtype=jnp.float32),
            jnp.arange(hidden.shape[0], dtype=jnp.float32),
        ]
    )
    tables = (time_embeddings(input_weight.shape[1]), *rope_tables(positions))
    proj_own, tables = lax.optimization_barrier((proj_own, tables))

    proj_slots = round_ring(proj_own)
    proj_pieces = proj_slots + over(proj_slots)
    proj_pieces = proj_pieces + swap(proj_pieces)
    out_own = jnp.concatenate([expert_output] + over([expert_output]), 0)
    out_pieces = round_ring(out_own)
    out_pieces = out_pieces + swap(out_pieces)

    corner_part, twin_part = project(
        from_corner, from_twin, key_pieces, value_pieces, columns
    )
    core_part, own_part = project(from_core, kept, key_pieces, value_pieces, columns)
    corner_paired = lax.ppermute(corner_part, "wide", beside)
    twin_sum = (twin_part + corner_paired).astype(jnp.bfloat16)
    twinned = lax.ppermute(twin_sum, "groups", facing)
    sums = (own_part, lax.ppermute(core_part, "wide", beside), twinned)

    span, width = action_noise.shape[1:]
    last = columns - 1
    proj_all = {
        (k // (2 * columns), k % (2 * columns)): piece for k, piece in enumerate(proj_pieces)
    }
    out_all = {(k // columns, k % columns): piece for k, piece in enumerate(out_pieces)}
    split = lambda pieces, ends: {
        key: piece for key, piece in pieces.items() if (key[1] % columns == last) == ends
    }
    prefix_tables = tables[1:]
    prefix_keys, prefix_values = cache(*prefix_tables, row_scale, sums, rows)
    proj, mix, *constants = prepare(
        (action_noise[0].T, input_weight, output_weight.T),
        split(proj_all, False),
        split(out_all, False),
        proj_own.shape[0] * wide_count,
        expert_output.shape[0] * wide_count,
        columns,
        rows,
        span,
    )
    actions = expert(
        prefix_lengths,
        (tables[0], expert_gain[None, :], final_gain[None, :], *prefix_tables),
        (proj, mix, prefix_keys, prefix_values, *constants),
        split(proj_all, True),
        split(out_all, True),
        columns,
        hidden.shape[0],
        width,
        span,
    )
    return actions.T[None]


def solution(mesh):
    placed = (
        P(("groups", "wide"), None, None),
        P(("groups", "wide")),
        P(("groups", "wide"), None, None),
        P(),
        P("wide", None),
        P("wide", None),
        P(),
        P(),
        P("wide", None),
        P("wide", None),
        P("wide", None),
        P("wide", None),
        P(),
        P(),
    )

    def whole(*arrays):
        return shards(
            *arrays, group_count=mesh.shape["groups"], wide_count=mesh.shape["wide"]
        )

    return jax.shard_map(
        whole,
        mesh=mesh,
        in_specs=placed,
        out_specs=P(("groups", "wide"), None, None),
        check_vma=False,
    )
```
